512 devices in a mesh: outer: 16 (over y, core), inner: 32 (over x, z).
Axes of the slice: x: 4, y: 8, z: 8, core: 2. Of those that a mesh axis runs over, the one named last changes fastest.
Arguments:
- queries: bfloat16 [32768, 4096], P('inner', 'outer'), may hold values from -150 to 150
- keys: bfloat16 [32768, 4096], P('inner', 'outer'), may hold values from -7 to 7
- values: bfloat16 [32768, 4096], P('inner', 'outer'), may hold values from -18 to 18
- counts: int32 [256], P('inner'), may hold values from 1 to 128, 24576 in all
- window_mask: int32 [256, 3], P('inner'), may hold values 0 or 1
- norm_gain: float32 [4096], P('outer'), may hold values from 0.5 to 1.5
Outputs:
- attended: bfloat16 [32768, 4096], P('inner', 'outer')
The draws below stay inside these ranges and needn't reach their ends.
Inputs may be any that keep to these rules, and one draw needn't show every extreme that they name: `counts`: the largest count is exactly 128.
All inputs are finite; a program needn't handle non-finite values. No bound on the sum of `counts` or of `window_mask` on one device may be relied on, other than what follows from the above.
Results may differ from the reference program's by a relative error of at most 0.0048.
Values may be sent and summed in bfloat16 or wider, within the bound.
A program may use at most 64 MiB of HBM per device.

```python
import math
import jax
import jax.numpy as jnp
import numpy as np
from jax import lax

HEADS = 32
HD = 128
BLK = 128
PREV = 3
WIDTH = 4096
SEQ = 32768
NBLK = 256


def key_field(key):
    base = jnp.clip(jax.random.normal(jax.random.fold_in(key, 11), (SEQ, WIDTH), jnp.float32), -6.0, 6.0)
    return base


def draw_keys(key, part):
    return key_field(key).astype(jnp.bfloat16)


def draw_queries(key, part):
    base = jnp.clip(jax.random.normal(jax.random.fold_in(key, 21), (SEQ, WIDTH), jnp.float32), -6.0, 6.0)
    return base.astype(jnp.bfloat16)


def draw_values(key, part):
    head_index = (jnp.arange(WIDTH) // HD).astype(jnp.float32)
    head_scale = jnp.exp(jnp.log(3.0) * head_index / max(HEADS - 1, 1))
    base = jnp.clip(jax.random.normal(jax.random.fold_in(key, 32), (SEQ, WIDTH), jnp.float32), -6.0, 6.0)
    return (base * head_scale[None, :]).astype(jnp.bfloat16)


def with_ends(array, stream_key, smallest, top_value):
    extent = array.shape
    spot = [jax.random.randint(jax.random.fold_in(stream_key, axis), (), 0, extent[axis]) for axis in range(len(extent))]
    array = array.at[tuple(spot)].set(smallest)
    longest = extent.index(max(extent))
    spot[longest] = (spot[longest] + 1) % extent[longest]
    return array.at[tuple(spot)].set(top_value)


def levels(own_key, extent, cuts, low, high):
    loudness = 1.0
    for dim, shards_of in cuts:
        heights = jax.random.uniform(jax.random.fold_in(jax.random.fold_in(own_key, 6), dim), (shards_of,), jnp.float32, low / len(cuts), high / len(cuts))
        loudness = loudness * jnp.repeat(jnp.exp(heights), extent[dim] // shards_of).reshape((-1,) + (1,) * (len(extent) - 1 - dim))
    return loudness


def profile(amount, total, bound, lean):
    loads = [(1 << 20) // math.isqrt(standing ** lean) + 1 for standing in range(2, amount + 1)]
    surplus, given = total - bound - (amount - 1), [1] * (amount - 1)
    while surplus > 0:
        candidates = [i for i in range(amount - 1) if given[i] < bound]
        pool, left = sum([loads[i] for i in candidates]), surplus
        for i in candidates:
            extra = min(bound - given[i], max(1, left * loads[i] // pool), surplus)
            given[i] = given[i] + extra
            surplus = surplus - extra
    return np.array([bound] + given)


def uneven_parts(rng, count, total, reach, lean):
    if count == 2:
        one = jax.random.randint(rng, (), max(1, total - reach), min(reach, total - 1) + 1)
        return jnp.stack([one, total - one])
    lengths = jnp.asarray(profile(count, total, reach, lean), jnp.int32)
    couples = (count - 1) // 2
    giver, taker = lengths[1:1 + 2 * couples:2], lengths[2:2 + 2 * couples:2]
    room = jnp.minimum(giver - 1, reach - taker)
    shifted = jax.random.randint(jax.random.fold_in(rng, 1), (couples,), 0, 1 << 20) % (room + 1)
    lengths = lengths.at[1:1 + 2 * couples:2].set(giver - shifted).at[2:2 + 2 * couples:2].set(taker + shifted)
    return lengths[jax.random.permutation(jax.random.fold_in(rng, 2), count)]


def setup_inputs(seed: int = 0) -> dict:
    splits = jax.random.split(jax.random.key(seed), 7)
    queries = draw_queries(jax.random.fold_in(splits[6], 71), 0)
    keys = draw_keys(jax.random.fold_in(splits[6], 71), 0)
    values = draw_values(jax.random.fold_in(splits[6], 71), 0)
    counts = uneven_parts(splits[3], NBLK, (3 * BLK // 4) * NBLK, BLK, 1).astype(jnp.int32)
    window_mask = with_ends((jax.random.randint(splits[4], (NBLK, PREV), 0, 3) < 2).astype(jnp.int32), jax.random.fold_in(splits[4], 1), 0, 1)
    norm_gain = jnp.clip(0.5 + 1.0 * jax.random.uniform(splits[5], (WIDTH,), jnp.float32) ** levels(splits[5], (WIDTH,), ((0, 16),), -0.2, 0.2), 0.5, 1.5)
    return dict(queries=queries, keys=keys, values=values, counts=counts, window_mask=window_mask, norm_gain=norm_gain)


def reference(queries, keys, values, counts, window_mask, norm_gain):
    heads_count = HEADS
    query_blocks = queries.reshape(NBLK, BLK, heads_count, HD)
    value_blocks = values.reshape(NBLK, BLK, heads_count, HD)
    position = jnp.arange(BLK, dtype=jnp.int32)
    key_valid = position[None, :] < counts[:, None]
    masked_keys = jnp.where(key_valid[:, :, None, None], keys.reshape(NBLK, BLK, heads_count, HD), jnp.zeros((), jnp.bfloat16)).astype(jnp.bfloat16)
    padded_keys = jnp.concatenate([jnp.zeros((PREV, BLK, heads_count, HD), jnp.bfloat16), masked_keys], axis=0)
    padded_values = jnp.concatenate([jnp.zeros((PREV, BLK, heads_count, HD), jnp.bfloat16), value_blocks], axis=0)
    padded_valid = jnp.concatenate([jnp.zeros((PREV, BLK), jnp.bool_), key_valid], axis=0)
    causal = position[:, None] >= position[None, :]
    causal_full = jnp.concatenate([jnp.ones((BLK, PREV * BLK), jnp.bool_), causal], axis=1)
    score_scale = 1.0 / HD ** 0.5
    gain_heads = norm_gain.reshape(heads_count, HD)

    def block_step(carried, index):
        query_here = lax.dynamic_index_in_dim(query_blocks, index, 0, keepdims=False).astype(jnp.float32)
        key_here = lax.dynamic_index_in_dim(masked_keys, index, 0, keepdims=False).astype(jnp.float32)
        value_here = lax.dynamic_index_in_dim(value_blocks, index, 0, keepdims=False).astype(jnp.float32)
        window_keys = lax.dynamic_slice_in_dim(padded_keys, index, PREV + 1, 0).reshape((PREV + 1) * BLK, heads_count, HD).astype(jnp.float32)
        window_values = lax.dynamic_slice_in_dim(padded_values, index, PREV + 1, 0).reshape((PREV + 1) * BLK, heads_count, HD).astype(jnp.float32)
        window_valid = lax.dynamic_slice_in_dim(padded_valid, index, PREV + 1, 0)
        mask_row = lax.dynamic_index_in_dim(window_mask, index, 0, keepdims=False)
        group_on = jnp.concatenate([mask_row[::-1] == 1, jnp.ones((1,), jnp.bool_)])
        allowed = (window_valid & group_on[:, None]).reshape(1, (PREV + 1) * BLK) & causal_full
        scores = jnp.einsum('thd,shd->hts', query_here, window_keys) * score_scale
        scores = jnp.where(allowed[None], scores, -1e+30)
        largest = lax.optimization_barrier(jnp.max(scores, axis=-1, keepdims=True))
        expd = jnp.exp(scores - largest)
        weights = (expd / lax.optimization_barrier(jnp.sum(expd, axis=-1, keepdims=True))).astype(jnp.bfloat16)
        local_part = jnp.einsum('hts,shd->thd', weights.astype(jnp.float32), window_values)
        prior_rounded = carried.astype(jnp.bfloat16).astype(jnp.float32)
        inter = jnp.einsum('thd,hde->the', query_here, prior_rounded)
        intra_weights = jnp.einsum('thd,shd->hts', query_here, key_here)
        intra_weights = jnp.where(causal[None], intra_weights, 0.0).astype(jnp.bfloat16)
        intra = jnp.einsum('hts,she->the', intra_weights.astype(jnp.float32), value_here)
        linear_part = inter + intra
        row_squares = lax.optimization_barrier(jnp.sum(linear_part * linear_part, axis=(1, 2), keepdims=True))
        normed = linear_part * lax.rsqrt(row_squares / WIDTH + 1e-06)
        result = (normed * gain_heads[None] + local_part).astype(jnp.bfloat16)
        updated = carried + jnp.einsum('shd,she->hde', key_here, value_here)
        return (updated, result.reshape(BLK, heads_count * HD))
    start = jnp.zeros((heads_count, HD, HD), jnp.float32)
    _, blocks_out = lax.scan(block_step, start, jnp.arange(NBLK, dtype=jnp.int32))
    return blocks_out.reshape(SEQ, heads_count * HD)
```

```python
import functools

import jax
import jax.numpy as jnp
from jax import lax
from jax.experimental import pallas as pl
from jax.experimental.pallas import tpu as pltpu
from jax.sharding import PartitionSpec as P

HD = 128
BLK = 128
PREV = 3
MESH = pl.DeviceIdType.MESH
NEG = -1e30
LOG2E = 1.4426950408889634


def dot_nt(a, b):
    return lax.dot_general(a, b, (((1,), (1,)), ((), ())), preferred_element_type=jnp.float32)


def dot_tn(a, b):
    return lax.dot_general(a, b, (((0,), (0,)), ((), ())), preferred_element_type=jnp.float32)


def dot_nn(a, b):
    return lax.dot_general(a, b, (((1,), (0,)), ((), ())), preferred_element_type=jnp.float32)


def kernel(
    ni,
    no,
    groups,
    heads,
    split,
    counts_ref,
    mask_ref,
    gain_ref,
    q_hbm,
    k_hbm,
    v_hbm,
    o_hbm,
    q_all,
    k_ext,
    v_ext,
    within,
    total,
    parts,
    prefixes,
    before,
    bias,
    rim_out,
    rim_in,
    lin,
    local,
    squares,
    all_squares,
    scale,
    out,
    load_sem,
    store_sem,
    parts_send,
    parts_recv,
    prefix_send,
    prefix_recv,
    rim_send,
    rim_recv,
    square_send,
    square_recv,
):
    rim = PREV * BLK
    span = groups * BLK
    width = no * heads * HD
    here = lax.axis_index("inner")
    stripe = lax.axis_index("outer")
    following = lax.rem(here + 1, ni)

    loads = [
        pltpu.make_async_copy(k_hbm, k_ext.at[pl.ds(rim, span)], load_sem.at[0]),
        pltpu.make_async_copy(v_hbm, v_ext.at[pl.ds(rim, span)], load_sem.at[1]),
        pltpu.make_async_copy(q_hbm, q_all, load_sem.at[2]),
    ]
    for load in loads:
        load.start()

    barrier = pltpu.get_barrier_semaphore()

    @pl.loop(1, ni)
    def _(step):
        pl.semaphore_signal(
            barrier, inc=1, device_id={"inner": lax.rem(here + step, ni)}, device_id_type=MESH
        )

    @pl.loop(1, no)
    def _(step):
        pl.semaphore_signal(
            barrier, inc=1, device_id={"outer": lax.rem(stripe + step, no)}, device_id_type=MESH
        )

    lane = lax.broadcasted_iota(jnp.int32, (1, BLK), 1)
    for g in range(groups):
        bias[pl.ds(g, 1), :] = jnp.where(lane < counts_ref[g], 0.0, NEG)
    rim_out[...] = jnp.full(rim_out.shape, NEG, jnp.float32)
    for j in range(PREV):
        rim_out[pl.ds(j, 1), :] = bias[pl.ds(groups - PREV + j, 1), :]

    loads[0].wait()
    loads[1].wait()
    token = lax.broadcasted_iota(jnp.int32, (BLK, HD), 0)
    for h in range(heads):
        cols = pl.ds(h * HD, HD)
        running = jnp.zeros((HD, HD), jnp.float32)
        for g in range(groups):
            rows = pl.ds(rim + g * BLK, BLK)
            masked = jnp.where(token < counts_ref[g], k_ext[rows, cols], jnp.zeros((), jnp.bfloat16))
            within[g, cols, :] = running
            running = running + dot_tn(masked, v_ext[rows, cols])
        piece = heads * HD // ni
        each = ni // heads
        total[pl.ds(h * each, each)] = running.reshape(each, piece, HD)
    parts[pl.ds(here, 1)] = total[pl.ds(here, 1)]

    pl.semaphore_wait(barrier, ni - 1 + no - 1)

    @pl.loop(1, ni)
    def _(step):
        there = lax.rem(here + step, ni)
        pltpu.make_async_remote_copy(
            src_ref=total.at[there],
            dst_ref=parts.at[here],
            send_sem=parts_send,
            recv_sem=parts_recv,
            device_id={"inner": there},
            device_id_type=MESH,
        ).start()

    rims = [
        pltpu.make_async_remote_copy(
            src_ref=source,
            dst_ref=target,
            send_sem=rim_send.at[n],
            recv_sem=rim_recv.at[n],
            device_id={"inner": following},
            device_id_type=MESH,
        )
        for n, (source, target) in enumerate(
            (
                (rim_out, rim_in),
                (k_ext.at[pl.ds(span, rim)], k_ext.at[pl.ds(0, rim)]),
                (v_ext.at[pl.ds(span, rim)], v_ext.at[pl.ds(0, rim)]),
            )
        )
    ]
    for copy in rims:
        copy.start()

    loads[2].wait()
    causal = lax.broadcasted_iota(jnp.int32, (BLK, BLK), 0) >= lax.broadcasted_iota(
        jnp.int32, (BLK, BLK), 1
    )
    factor = LOG2E / HD**0.5

    def intra(g, scores, h):
        valid = causal & (bias[pl.ds(g, 1), :] == 0.0)
        weights = jnp.where(valid, scores, 0.0).astype(jnp.bfloat16)
        rows = pl.ds(g * BLK, BLK)
        lin[rows, pl.ds(h * HD, HD)] = dot_nn(
            weights, v_ext[pl.ds(rim + g * BLK, BLK), pl.ds(h * HD, HD)]
        )

    def window(g, earlier, with_intra):
        rows = pl.ds(g * BLK, BLK)
        for h in range(heads):
            cols = pl.ds(h * HD, HD)
            keys = pl.ds(g * BLK, (PREV + 1) * BLK)
            scores = dot_nt(q_all[rows, cols], k_ext[keys, cols])
            own = scores[:, PREV * BLK :]
            if with_intra:
                intra(g, own, h)
            seen = [scores[:, j * BLK : (j + 1) * BLK] + earlier[j] for j in range(PREV)]
            seen.append(jnp.where(causal, own + bias[pl.ds(g, 1), :], NEG))
            largest = functools.reduce(jnp.maximum, seen)
            largest = jnp.max(largest, axis=-1, keepdims=True)
            expd = [jnp.exp2((s - largest) * factor) for s in seen]
            denominator = jnp.sum(functools.reduce(jnp.add, expd), axis=-1, keepdims=True)
            inverse = 1.0 / denominator
            weights = jnp.concatenate([(e * inverse).astype(jnp.bfloat16) for e in expd], axis=1)
            local[rows, cols] = dot_nn(weights, v_ext[keys, cols])

    def switch(g, j):
        return jnp.where(mask_ref[g, PREV - 1 - j] == 1, 0.0, NEG)

    def inner_window(g):
        window(g, [bias[pl.ds(g - PREV + j, 1), :] + switch(g, j) for j in range(PREV)], True)

    @pl.loop(PREV, split)
    def _(g):
        inner_window(g)

    def arrived(buffer, send, recv, count):
        return pltpu.make_async_remote_copy(
            src_ref=buffer.at[pl.ds(0, count)],
            dst_ref=buffer.at[pl.ds(0, count)],
            send_sem=send,
            recv_sem=recv,
            device_id={"inner": following},
            device_id_type=MESH,
        )

    arrived(parts, parts_send, parts_recv, ni - 1).wait_recv()
    so_far = jnp.zeros(parts.shape[1:], jnp.float32)
    for n in range(ni):
        prefixes[n] = so_far
        so_far = so_far + parts[n]
    before[pl.ds(here, 1)] = prefixes[pl.ds(here, 1)]

    @pl.loop(1, ni)
    def _(step):
        there = lax.rem(here + step, ni)
        pltpu.make_async_remote_copy(
            src_ref=prefixes.at[there],
            dst_ref=before.at[here],
            send_sem=prefix_send,
            recv_sem=prefix_recv,
            device_id={"inner": there},
            device_id_type=MESH,
        ).start()

    @pl.loop(split, groups)
    def _(g):
        inner_window(g)

    @pl.loop(0, PREV)
    def _(g):
        for h in range(heads):
            cols = pl.ds(h * HD, HD)
            intra(
                g,
                dot_nt(q_all[pl.ds(g * BLK, BLK), cols], k_ext[pl.ds(rim + g * BLK, BLK), cols]),
                h,
            )

    arrived(before, prefix_send, prefix_recv, ni - 1).wait_recv()

    @pl.loop(0, groups)
    def _(g):
        rows = pl.ds(g * BLK, BLK)
        powers = jnp.zeros((BLK, HD), jnp.float32)
        for h in range(heads):
            cols = pl.ds(h * HD, HD)
            each = ni // heads
            carried = before[pl.ds(h * each, each)].reshape(HD, HD)
            prior = (carried + within[g, cols, :]).astype(jnp.bfloat16)
            whole = lin[rows, cols] + dot_nn(q_all[rows, cols], prior)
            lin[rows, cols] = whole
            powers = powers + whole * whole
        squares[pl.ds(g, 1), :] = jnp.sum(powers.T, axis=0, keepdims=True)

    all_squares[pl.ds(stripe, 1)] = squares[...][None]

    @pl.loop(1, no)
    def _(step):
        there = lax.rem(stripe + step, no)
        pltpu.make_async_remote_copy(
            src_ref=squares,
            dst_ref=all_squares.at[stripe],
            send_sem=square_send,
            recv_sem=square_recv,
            device_id={"outer": there},
            device_id_type=MESH,
        ).start()

    for copy in rims:
        copy.wait_recv()
    first = jnp.where(here == 0, NEG, 0.0)

    @pl.loop(0, PREV)
    def _(g):
        earlier = []
        for j in range(PREV):
            row = g - PREV + j
            behind = rim_in[pl.ds(jnp.minimum(row + PREV, PREV), 1), :] + first
            inside = bias[pl.ds(jnp.maximum(row, 0), 1), :]
            earlier.append(jnp.where(row < 0, behind, inside) + switch(g, j))
        window(g, earlier, False)

    arrived(all_squares, square_send, square_recv, no - 1).wait_recv()
    row_squares = jnp.sum(all_squares[...], axis=0)
    scale[...] = lax.rsqrt(row_squares / width + 1e-6)

    @pl.loop(0, groups)
    def _(g):
        rows = pl.ds(g * BLK, BLK)
        by_token = jnp.broadcast_to(scale[pl.ds(g, 1), :], (HD, BLK)).T
        for h in range(heads):
            cols = pl.ds(h * HD, HD)
            normed = lin[rows, cols] * by_token
            out[rows, cols] = (normed * gain_ref[:, cols] + local[rows, cols]).astype(jnp.bfloat16)

    store = pltpu.make_async_copy(out, o_hbm, store_sem)
    store.start()
    arrived(total, parts_send, parts_recv, ni - 1).wait_send()
    arrived(prefixes, prefix_send, prefix_recv, ni - 1).wait_send()
    arrived(all_squares, square_send, square_recv, no - 1).wait_send()
    for copy in rims:
        copy.wait_send()
    store.wait()


def shards(ni, no, queries, keys, values, counts, window_mask, norm_gain):
    span, wide = queries.shape
    groups, heads = span // BLK, wide // HD
    piece = heads * HD // ni
    rim = PREV * BLK
    any_space = pl.BlockSpec(memory_space=pl.ANY)
    dma = pltpu.SemaphoreType.DMA
    f32, bf16 = jnp.float32, jnp.bfloat16
    return pl.pallas_call(
        functools.partial(kernel, ni, no, groups, heads, min(groups, PREV + 3)),
        out_shape=jax.ShapeDtypeStruct((span, wide), bf16),
        in_specs=[
            pl.BlockSpec(memory_space=pltpu.SMEM),
            pl.BlockSpec(memory_space=pltpu.SMEM),
            pl.BlockSpec(memory_space=pltpu.VMEM),
            any_space,
            any_space,
            any_space,
        ],
        out_specs=any_space,
        scratch_shapes=[
            pltpu.VMEM((span, wide), bf16),
            pltpu.VMEM((rim + span, wide), bf16),
            pltpu.VMEM((rim + span, wide), bf16),
            pltpu.VMEM((groups, heads * HD, HD), f32),
            pltpu.VMEM((ni, piece, HD), f32),
            pltpu.VMEM((ni, piece, HD), f32),
            pltpu.VMEM((ni, piece, HD), f32),
            pltpu.VMEM((ni, piece, HD), f32),
            pltpu.VMEM((groups, BLK), f32),
            pltpu.VMEM((8, BLK), f32),
            pltpu.VMEM((8, BLK), f32),
            pltpu.VMEM((span, wide), f32),
            pltpu.VMEM((span, wide), f32),
            pltpu.VMEM((groups, BLK), f32),
            pltpu.VMEM((no, groups, BLK), f32),
            pltpu.VMEM((groups, BLK), f32),
            pltpu.VMEM((span, wide), bf16),
            dma((3,)),
            dma,
            dma,
            dma,
            dma,
            dma,
            dma((3,)),
            dma((3,)),
            dma,
            dma,
        ],
        compiler_params=pltpu.CompilerParams(
            collective_id=0, has_side_effects=True, vmem_limit_bytes=48 * 2**20
        ),
        name="layer",
    )(counts, window_mask, norm_gain.reshape(1, wide), queries, keys, values)


def solution(mesh):
    return jax.shard_map(
        functools.partial(shards, mesh.shape["inner"], mesh.shape["outer"]),
        mesh=mesh,
        in_specs=(
            P("inner", "outer"),
            P("inner", "outer"),
            P("inner", "outer"),
            P("inner"),
            P("inner", None),
            P("outer"),
        ),
        out_specs=P("inner", "outer"),
        check_vma=False,
    )
```

```python
import functools

import jax
import jax.numpy as jnp
from jax import lax
from jax.experimental import pallas as pl
from jax.experimental.pallas import tpu as pltpu
from jax.sharding import PartitionSpec as P

HD = 128
BLK = 128
PREV = 3
LOADS = 4
MESH = pl.DeviceIdType.MESH
NEG = -1e30
LOG2E = 1.4426950408889634


def torus(sizes):
    def hops(step):
        return sum(min(s, n - s) for s, n in zip(step, sizes))

    steps = [()]
    for n in sizes:
        steps = [(*step, s) for step in steps for s in range(n)]
    return sorted(steps[1:], key=hops, reverse=True)


def moved(place, step, sizes):
    index, stride = 0, 1
    for s, n in zip(reversed(step), reversed(sizes)):
        digit = lax.rem(place // stride, n) if stride > 1 else lax.rem(place, n)
        index = index + lax.rem(digit + s, n) * stride
        stride *= n
    return index


def dot_nt(a, b):
    return lax.dot_general(a, b, (((1,), (1,)), ((), ())), preferred_element_type=jnp.float32)


def dot_tn(a, b):
    return lax.dot_general(a, b, (((0,), (0,)), ((), ())), preferred_element_type=jnp.float32)


def dot_nn(a, b):
    return lax.dot_general(a, b, (((1,), (0,)), ((), ())), preferred_element_type=jnp.float32)


def kernel(
    ni,
    no,
    groups,
    heads,
    counts_hbm,
    mask_hbm,
    gain_hbm,
    q_hbm,
    k_hbm,
    v_hbm,
    o_hbm,
    counts_ref,
    mask_ref,
    gain_ref,
    q_all,
    k_ext,
    v_ext,
    within,
    total,
    parts,
    prefixes,
    before,
    bias,
    rim_out,
    rim_in,
    lin,
    local,
    squares,
    all_squares,
    scale,
    out,
    small_sem,
    load_sem,
    store_sem,
    parts_send,
    parts_recv,
    prefix_send,
    prefix_recv,
    rim_send,
    rim_recv,
    square_send,
    square_recv,
    ready,
):
    rim = PREV * BLK
    span = groups * BLK
    width = no * heads * HD
    here = lax.axis_index("inner")
    stripe = lax.axis_index("outer")
    following = lax.rem(here + 1, ni)

    small = [
        pltpu.make_async_copy(counts_hbm, counts_ref, small_sem.at[0]),
        pltpu.make_async_copy(mask_hbm, mask_ref, small_sem.at[1]),
        pltpu.make_async_copy(gain_hbm, gain_ref, small_sem.at[2]),
    ]
    chunk = span // LOADS
    loads = []
    for n in range(LOADS):
        rows, ext = pl.ds(n * chunk, chunk), pl.ds(rim + n * chunk, chunk)
        loads.append(pltpu.make_async_copy(k_hbm.at[rows], k_ext.at[ext], load_sem.at[2 * n]))
        loads.append(pltpu.make_async_copy(v_hbm.at[rows], v_ext.at[ext], load_sem.at[2 * n + 1]))
    load_q = pltpu.make_async_copy(q_hbm, q_all, load_sem.at[2 * LOADS])
    small[0].start()
    for load in loads:
        load.start()
    small[1].start()
    small[2].start()
    load_q.start()

    barrier = pltpu.get_barrier_semaphore()
    inner_sizes = (4, 8) if ni == 32 else (ni,)
    outer_sizes = (8, 2) if no == 16 else (no,)
    inner_peers = [{"inner": moved(here, step, inner_sizes)} for step in torus(inner_sizes)]
    outer_peers = [{"outer": moved(stripe, step, outer_sizes)} for step in torus(outer_sizes)]
    line = inner_sizes[-1]
    half = line // 2
    owners = ni // 2

    def owns(place):
        return lax.rem(place, line) < half

    def rank(place):
        return place // line * half + lax.rem(place, line)

    owner = owns(here)
    preceding = lax.rem(here + ni - 1, ni)

    @pl.when(owner)
    def _():
        for peer in inner_peers:
            pl.semaphore_signal(barrier, inc=1, device_id=peer, device_id_type=MESH)

    @pl.when(jnp.logical_not(owner))
    def _():
        pl.semaphore_signal(barrier, inc=1, device_id={"inner": preceding}, device_id_type=MESH)

    for peer in outer_peers:
        pl.semaphore_signal(barrier, inc=1, device_id=peer, device_id_type=MESH)

    small[0].wait()
    lane = lax.broadcasted_iota(jnp.int32, (1, BLK), 1)
    for g in range(groups):
        bias[pl.ds(g, 1), :] = jnp.where(lane < counts_ref[g], 0.0, NEG)
    rim_out[...] = jnp.full(rim_out.shape, NEG, jnp.float32)
    for j in range(PREV):
        rim_out[pl.ds(j, 1), :] = bias[pl.ds(groups - PREV + j, 1), :]

    token = lax.broadcasted_iota(jnp.int32, (BLK, HD), 0)
    each = owners // heads
    piece = heads * HD // owners
    running = [jnp.zeros((HD, HD), jnp.float32)] * heads
    for g in range(groups):
        if (g * BLK) % chunk == 0:
            loads[2 * (g * BLK // chunk)].wait()
            loads[2 * (g * BLK // chunk) + 1].wait()
        for h in range(heads):
            cols = pl.ds(h * HD, HD)
            rows = pl.ds(rim + g * BLK, BLK)
            masked = jnp.where(token < counts_ref[g], k_ext[rows, cols], jnp.zeros((), jnp.bfloat16))
            if g:
                within[g, cols, :] = running[h].astype(jnp.bfloat16)
            running[h] = running[h] + dot_tn(masked, v_ext[rows, cols])
    for h in range(heads):
        total[pl.ds(h * each, each)] = running[h].reshape(each, piece, HD).astype(jnp.bfloat16)
    within[0] = jnp.zeros(within.shape[1:], jnp.bfloat16)

    pl.semaphore_wait(
        barrier,
        no - 1 + owners - jnp.where(owner, 1, 0) + jnp.where(owns(following), 0, 1),
    )

    def send_part(peer):
        there = peer["inner"]

        @pl.when(owns(there))
        def _():
            pltpu.make_async_remote_copy(
                src_ref=total.at[rank(there)],
                dst_ref=parts.at[here],
                send_sem=parts_send,
                recv_sem=parts_recv,
                device_id=peer,
                device_id_type=MESH,
            ).start()

    for peer in inner_peers:
        send_part(peer)

    rims = [
        pltpu.make_async_remote_copy(
            src_ref=source,
            dst_ref=target,
            send_sem=rim_send.at[n],
            recv_sem=rim_recv.at[n],
            device_id={"inner": following},
            device_id_type=MESH,
        )
        for n, (source, target) in enumerate(
            (
                (rim_out, rim_in),
                (k_ext.at[pl.ds(span, rim)], k_ext.at[pl.ds(0, rim)]),
                (v_ext.at[pl.ds(span, rim)], v_ext.at[pl.ds(0, rim)]),
            )
        )
    ]
    first, last = here == 0, here == ni - 1

    @pl.when(jnp.logical_not(last))
    def _():
        for copy in rims:
            copy.start()

    @pl.when(first)
    def _():
        rim_in[...] = jnp.full(rim_in.shape, NEG, jnp.float32)
        k_ext[pl.ds(0, rim)] = jnp.zeros((rim, k_ext.shape[1]), jnp.bfloat16)
        v_ext[pl.ds(0, rim)] = jnp.zeros((rim, v_ext.shape[1]), jnp.bfloat16)

    @pl.when(jnp.logical_not(owner))
    def _():
        for n in range(owners):
            pl.semaphore_signal(
                ready,
                inc=1,
                device_id={"inner": n // half * line + n % half},
                device_id_type=MESH,
            )

    load_q.wait()
    small[1].wait()
    causal = lax.broadcasted_iota(jnp.int32, (BLK, BLK), 0) >= lax.broadcasted_iota(
        jnp.int32, (BLK, BLK), 1
    )
    factor = LOG2E / HD**0.5

    def intra(g, scores, h):
        valid = causal & (bias[pl.ds(g, 1), :] == 0.0)
        weights = jnp.where(valid, scores, 0.0).astype(jnp.bfloat16)
        rows, cols = pl.ds(g * BLK, BLK), pl.ds(h * HD, HD)
        lin[rows, cols] = dot_nn(weights, v_ext[pl.ds(rim + g * BLK, BLK), cols]) + dot_nn(
            q_all[rows, cols], within[g, cols, :]
        )

    def window(g, earlier, with_intra):
        rows = pl.ds(g * BLK, BLK)
        for h in range(heads):
            cols = pl.ds(h * HD, HD)
            keys = pl.ds(g * BLK, (PREV + 1) * BLK)
            scores = dot_nt(q_all[rows, cols], k_ext[keys, cols])
            own = scores[:, PREV * BLK :]
            if with_intra:
                intra(g, own, h)
            seen = [scores[:, j * BLK : (j + 1) * BLK] + earlier[j] for j in range(PREV)]
            seen.append(jnp.where(causal, own + bias[pl.ds(g, 1), :], NEG))
            largest = functools.reduce(jnp.maximum, seen)
            largest = jnp.max(largest, axis=-1, keepdims=True)
            expd = [jnp.exp2((s - largest) * factor) for s in seen]
            denominator = jnp.sum(functools.reduce(jnp.add, expd), axis=-1, keepdims=True)
            inverse = 1.0 / denominator
            weights = jnp.concatenate([(e * inverse).astype(jnp.bfloat16) for e in expd], axis=1)
            local[rows, cols] = dot_nn(weights, v_ext[keys, cols])

    def switch(g, j):
        return jnp.where(mask_ref[PREV - 1 - j, g] == 1, 0.0, NEG)

    def inner_window(g):
        window(g, [bias[pl.ds(g - PREV + j, 1), :] + switch(g, j) for j in range(PREV)], True)

    @pl.loop(PREV, groups)
    def _(g):
        inner_window(g)

    def arrived(buffer, send, recv, count):
        return pltpu.make_async_remote_copy(
            src_ref=buffer.at[pl.ds(0, count)],
            dst_ref=buffer.at[pl.ds(0, count)],
            send_sem=send,
            recv_sem=recv,
            device_id={"inner": following},
            device_id_type=MESH,
        )

    @pl.loop(0, PREV)
    def _(g):
        for h in range(heads):
            cols = pl.ds(h * HD, HD)
            intra(
                g,
                dot_nt(q_all[pl.ds(g * BLK, BLK), cols], k_ext[pl.ds(rim + g * BLK, BLK), cols]),
                h,
            )

    @pl.when(owner)
    def _():
        parts[pl.ds(here, 1)] = total[pl.ds(rank(here), 1)]
        arrived(parts, parts_send, parts_recv, ni - 1).wait_recv()
        so_far = jnp.zeros(parts.shape[1:], jnp.float32)
        for n in range(ni):
            prefixes[n] = so_far.astype(jnp.bfloat16)
            so_far = so_far + parts[n].astype(jnp.float32)
        before[pl.ds(rank(here), 1)] = prefixes[pl.ds(here, 1)]
        pl.semaphore_wait(ready, ni - owners)
        for peer in inner_peers:
            pltpu.make_async_remote_copy(
                src_ref=prefixes.at[peer["inner"]],
                dst_ref=before.at[rank(here)],
                send_sem=prefix_send,
                recv_sem=prefix_recv,
                device_id=peer,
                device_id_type=MESH,
            ).start()


    @pl.when(owner)
    def _():
        arrived(before, prefix_send, prefix_recv, owners - 1).wait_recv()

    @pl.when(jnp.logical_not(owner))
    def _():
        arrived(before, prefix_send, prefix_recv, owners).wait_recv()


    carried = [
        before[pl.ds(h * each, each)].reshape(HD, HD) for h in range(heads)
    ]
    for g in range(groups):
        rows = pl.ds(g * BLK, BLK)
        powers = jnp.zeros((BLK, HD), jnp.float32)
        for h in range(heads):
            cols = pl.ds(h * HD, HD)
            whole = lin[rows, cols] + dot_nn(q_all[rows, cols], carried[h])
            lin[rows, cols] = whole
            powers = powers + whole * whole
        squares[pl.ds(g, 1), :] = jnp.sum(powers.T, axis=0, keepdims=True)

    all_squares[pl.ds(stripe, 1)] = squares[...][None]

    for peer in outer_peers:
        pltpu.make_async_remote_copy(
            src_ref=squares,
            dst_ref=all_squares.at[stripe],
            send_sem=square_send,
            recv_sem=square_recv,
            device_id=peer,
            device_id_type=MESH,
        ).start()


    @pl.when(jnp.logical_not(first))
    def _():
        for copy in rims:
            copy.wait_recv()

    @pl.loop(0, PREV)
    def _(g):
        earlier = []
        for j in range(PREV):
            row = g - PREV + j
            behind = rim_in[pl.ds(jnp.minimum(row + PREV, PREV), 1), :]
            inside = bias[pl.ds(jnp.maximum(row, 0), 1), :]
            earlier.append(jnp.where(row < 0, behind, inside) + switch(g, j))
        window(g, earlier, False)

    arrived(all_squares, square_send, square_recv, no - 1).wait_recv()
    row_squares = jnp.sum(all_squares[...], axis=0)
    scale[...] = lax.rsqrt(row_squares / width + 1e-6)

    small[2].wait()
    stores = []
    for g in range(groups):
        rows = pl.ds(g * BLK, BLK)
        by_token = jnp.broadcast_to(scale[pl.ds(g, 1), :], (HD, BLK)).T
        for h in range(heads):
            cols = pl.ds(h * HD, HD)
            normed = lin[rows, cols] * by_token
            out[rows, cols] = (normed * gain_ref[:, cols] + local[rows, cols]).astype(jnp.bfloat16)
        stores.append(pltpu.make_async_copy(out.at[rows], o_hbm.at[rows], store_sem.at[g]))
        stores[-1].start()


    @pl.when(owner)
    def _():
        arrived(total, parts_send, parts_recv, owners - 1).wait_send()
        arrived(prefixes, prefix_send, prefix_recv, ni - 1).wait_send()

    @pl.when(jnp.logical_not(owner))
    def _():
        arrived(total, parts_send, parts_recv, owners).wait_send()

    arrived(all_squares, square_send, square_recv, no - 1).wait_send()

    @pl.when(jnp.logical_not(last))
    def _():
        for copy in rims:
            copy.wait_send()

    for store in stores:
        store.wait()


def shards(ni, no, queries, keys, values, counts, window_mask, norm_gain):
    span, wide = queries.shape
    groups, heads = span // BLK, wide // HD
    owners = ni // 2
    piece = heads * HD // owners
    rim = PREV * BLK
    any_space = pl.BlockSpec(memory_space=pltpu.HBM)
    dma = pltpu.SemaphoreType.DMA
    f32, bf16 = jnp.float32, jnp.bfloat16
    return pl.pallas_call(
        functools.partial(kernel, ni, no, groups, heads),
        out_shape=jax.ShapeDtypeStruct((span, wide), bf16),
        in_specs=[any_space] * 6,
        out_specs=any_space,
        scratch_shapes=[
            pltpu.SMEM(counts.shape, jnp.int32),
            pltpu.SMEM(window_mask.shape[::-1], jnp.int32),
            pltpu.VMEM((1, wide), f32),
            pltpu.VMEM((span, wide), bf16),
            pltpu.VMEM((rim + span, wide), bf16),
            pltpu.VMEM((rim + span, wide), bf16),
            pltpu.VMEM((groups, heads * HD, HD), bf16),
            pltpu.VMEM((owners, piece, HD), bf16),
            pltpu.VMEM((ni, piece, HD), bf16),
            pltpu.VMEM((ni, piece, HD), bf16),
            pltpu.VMEM((owners, piece, HD), bf16),
            pltpu.VMEM((groups, BLK), f32),
            pltpu.VMEM((8, BLK), f32),
            pltpu.VMEM((8, BLK), f32),
            pltpu.VMEM((span, wide), f32),
            pltpu.VMEM((span, wide), f32),
            pltpu.VMEM((groups, BLK), f32),
            pltpu.VMEM((no, groups, BLK), f32),
            pltpu.VMEM((groups, BLK), f32),
            pltpu.VMEM((span, wide), bf16),
            dma((3,)),
            dma((2 * LOADS + 1,)),
            dma((groups,)),
            dma,
            dma,
            dma,
            dma,
            dma((3,)),
            dma((3,)),
            dma,
            dma,
            pltpu.SemaphoreType.REGULAR,
        ],
        compiler_params=pltpu.CompilerParams(
            collective_id=0, has_side_effects=True, vmem_limit_bytes=56 * 2**20
        ),
        name="layer",
    )(counts, window_mask.T, norm_gain.reshape(1, wide), queries, keys, values)


def solution(mesh):
    return jax.shard_map(
        functools.partial(shards, mesh.shape["inner"], mesh.shape["outer"]),
        mesh=mesh,
        in_specs=(
            P("inner", "outer"),
            P("inner", "outer"),
            P("inner", "outer"),
            P("inner"),
            P("inner", None),
            P("outer"),
        ),
        out_specs=P("inner", "outer"),
        check_vma=False,
    )
```

```python
import functools

import jax
import jax.numpy as jnp
from jax import lax
from jax.experimental import pallas as pl
from jax.experimental.pallas import tpu as pltpu
from jax.sharding import PartitionSpec as P

HD = 128
BLK = 128
PREV = 3
LOADS = 4
MESH = pl.DeviceIdType.MESH
NEG = -1e30
LOG2E = 1.4426950408889634


def torus(sizes):
    def hops(step):
        return sum(min(s, n - s) for s, n in zip(step, sizes))

    steps = [()]
    for n in sizes:
        steps = [(*step, s) for step in steps for s in range(n)]
    return sorted(steps[1:], key=hops, reverse=True)


def moved(place, step, sizes):
    index, stride = 0, 1
    for s, n in zip(reversed(step), reversed(sizes)):
        digit = lax.rem(place // stride, n) if stride > 1 else lax.rem(place, n)
        index = index + lax.rem(digit + s, n) * stride
        stride *= n
    return index


def dot_nt(a, b):
    return lax.dot_general(a, b, (((1,), (1,)), ((), ())), preferred_element_type=jnp.float32)


def dot_tn(a, b):
    return lax.dot_general(a, b, (((0,), (0,)), ((), ())), preferred_element_type=jnp.float32)


def dot_nn(a, b):
    return lax.dot_general(a, b, (((1,), (0,)), ((), ())), preferred_element_type=jnp.float32)


def kernel(
    ni,
    no,
    groups,
    heads,
    counts_hbm,
    mask_hbm,
    gain_hbm,
    q_hbm,
    k_hbm,
    v_hbm,
    o_hbm,
    counts_ref,
    mask_ref,
    gain_ref,
    q_all,
    k_ext,
    v_ext,
    within,
    total,
    parts,
    prefixes,
    before,
    bias,
    rim_out,
    rim_in,
    lin,
    local,
    squares,
    all_squares,
    scale,
    out,
    small_sem,
    load_sem,
    store_sem,
    parts_send,
    parts_recv,
    prefix_send,
    prefix_recv,
    rim_send,
    rim_recv,
    square_send,
    square_recv,
    ready,
    entered,
    go,
    relay_bias,
    relay_keys,
    relay_values,
    hop_send,
    hop_recv,
):
    rim = PREV * BLK
    span = groups * BLK
    width = no * heads * HD
    here = lax.axis_index("inner")
    stripe = lax.axis_index("outer")
    following = lax.rem(here + 1, ni)

    small = [
        pltpu.make_async_copy(counts_hbm, counts_ref, small_sem.at[0]),
        pltpu.make_async_copy(mask_hbm, mask_ref, small_sem.at[1]),
        pltpu.make_async_copy(gain_hbm, gain_ref, small_sem.at[2]),
    ]
    chunk = span // LOADS
    loads = []
    for n in range(LOADS):
        rows, ext = pl.ds(n * chunk, chunk), pl.ds(rim + n * chunk, chunk)
        loads.append(pltpu.make_async_copy(k_hbm.at[rows], k_ext.at[ext], load_sem.at[2 * n]))
        loads.append(pltpu.make_async_copy(v_hbm.at[rows], v_ext.at[ext], load_sem.at[2 * n + 1]))
    load_q = pltpu.make_async_copy(q_hbm, q_all, load_sem.at[2 * LOADS])
    small[0].start()
    for load in loads:
        load.start()
    small[1].start()
    small[2].start()
    load_q.start()

    barrier = pltpu.get_barrier_semaphore()
    inner_sizes = {32: (4, 8), 8: (2, 4)}.get(ni, (1, ni))
    outer_sizes = (8, 2) if no == 16 else (no,)
    inner_peers = [{"inner": moved(here, step, inner_sizes)} for step in torus(inner_sizes)]
    outer_peers = [{"outer": moved(stripe, step, outer_sizes)} for step in torus(outer_sizes)]
    line = inner_sizes[-1]
    half = line // 2
    owners = ni // 2

    def owns(place):
        return lax.rem(place, line) < half

    def rank(place):
        return place // line * half + lax.rem(place, line)

    owner = owns(here)
    preceding = lax.rem(here + ni - 1, ni)
    first, last = here == 0, here == ni - 1
    tail = lax.rem(here, line) == line - 1
    straight = jnp.logical_not(tail)
    detour = jnp.logical_and(tail, jnp.logical_not(last))
    relays = jnp.logical_and(tail, here >= line)
    ahead = lax.rem(here + line, ni)
    behind = lax.rem(here + ni - line, ni)
    head = here // line * line

    @pl.when(owner)
    def _():
        for peer in inner_peers:
            pl.semaphore_signal(barrier, inc=1, device_id=peer, device_id_type=MESH)

    @pl.when(jnp.logical_not(owner))
    def _():
        pl.semaphore_signal(barrier, inc=1, device_id={"inner": preceding}, device_id_type=MESH)

    @pl.when(relays)
    def _():
        pl.semaphore_signal(barrier, inc=1, device_id={"inner": behind}, device_id_type=MESH)

    hub = stripe == 0

    @pl.when(hub)
    def _():
        for peer in outer_peers:
            pl.semaphore_signal(barrier, inc=1, device_id=peer, device_id_type=MESH)

    small[0].wait()
    lane = lax.broadcasted_iota(jnp.int32, (1, BLK), 1)
    for g in range(groups):
        bias[pl.ds(g, 1), :] = jnp.where(lane < counts_ref[g], 0.0, NEG)
    rim_out[...] = jnp.full(rim_out.shape, NEG, jnp.float32)
    for j in range(PREV):
        rim_out[pl.ds(j, 1), :] = bias[pl.ds(groups - PREV + j, 1), :]

    greeters = (
        owners
        - jnp.where(owner, 1, 0)
        + jnp.where(owns(following), 0, 1)
        + jnp.where(detour, 1, 0)
        + jnp.where(hub, 0, 1)
    )
    rims = [(rim_out, rim_in, relay_bias)]
    for n in reversed(range(PREV)):
        for ext, relay in ((k_ext, relay_keys), (v_ext, relay_values)):
            near, far = pl.ds(n * BLK, BLK), pl.ds(span + n * BLK, BLK)
            rims.append((ext.at[far], ext.at[near], relay.at[near]))

    def push(n, source, target, send, recv, there):
        return pltpu.make_async_remote_copy(
            src_ref=source,
            dst_ref=target,
            send_sem=send.at[n],
            recv_sem=recv.at[n],
            device_id={"inner": there},
            device_id_type=MESH,
        )

    for load in loads:
        load.wait()

    @pl.when(detour)
    def _():
        pl.semaphore_wait(barrier, greeters)
        for n, (source, _, relay) in enumerate(rims):
            push(n, source, relay, rim_send, hop_recv, ahead).start()

    token = lax.broadcasted_iota(jnp.int32, (BLK, HD), 0)
    each = owners // heads
    piece = heads * HD // owners
    running = [jnp.zeros((HD, HD), jnp.float32)] * heads
    for g in range(groups):
        for h in range(heads):
            cols = pl.ds(h * HD, HD)
            rows = pl.ds(rim + g * BLK, BLK)
            masked = jnp.where(token < counts_ref[g], k_ext[rows, cols], jnp.zeros((), jnp.bfloat16))
            if g:
                within[g, cols, :] = running[h].astype(jnp.bfloat16)
            running[h] = running[h] + dot_tn(masked, v_ext[rows, cols])
    for h in range(heads):
        total[pl.ds(h * each, each)] = running[h].reshape(each, piece, HD).astype(jnp.bfloat16)
    within[0] = jnp.zeros(within.shape[1:], jnp.bfloat16)

    @pl.when(jnp.logical_not(detour))
    def _():
        pl.semaphore_wait(barrier, greeters)

    def send_part(peer):
        there = peer["inner"]

        @pl.when(owns(there))
        def _():
            pltpu.make_async_remote_copy(
                src_ref=total.at[rank(there)],
                dst_ref=parts.at[here],
                send_sem=parts_send,
                recv_sem=parts_recv.at[here // stage],
                device_id=peer,
                device_id_type=MESH,
            ).start()

    stage = max(1, ni // 8)
    stages = ni // stage

    @pl.when(jnp.logical_not(last))
    def _():
        for peer in inner_peers:
            send_part(peer)

    @pl.when(straight)
    def _():
        for n, (source, target, _) in enumerate(rims):
            push(n, source, target, rim_send, rim_recv, following).start()

    @pl.when(first)
    def _():
        rim_in[...] = jnp.full(rim_in.shape, NEG, jnp.float32)
        before[...] = jnp.zeros(before.shape, jnp.bfloat16)
        k_ext[pl.ds(0, rim)] = jnp.zeros((rim, k_ext.shape[1]), jnp.bfloat16)
        v_ext[pl.ds(0, rim)] = jnp.zeros((rim, v_ext.shape[1]), jnp.bfloat16)

    @pl.when(jnp.logical_not(hub))
    def _():
        pl.semaphore_signal(entered, inc=1, device_id={"outer": 0}, device_id_type=MESH)

    @pl.when(jnp.logical_not(owner))
    def _():
        for n in range(owners):
            pl.semaphore_signal(
                ready,
                inc=1,
                device_id={"inner": n // half * line + n % half},
                device_id_type=MESH,
            )

    load_q.wait()
    small[1].wait()
    causal = lax.broadcasted_iota(jnp.int32, (BLK, BLK), 0) >= lax.broadcasted_iota(
        jnp.int32, (BLK, BLK), 1
    )
    factor = LOG2E / HD**0.5

    def intra(g, scores, h):
        valid = causal & (bias[pl.ds(g, 1), :] == 0.0)
        weights = jnp.where(valid, scores, 0.0).astype(jnp.bfloat16)
        rows, cols = pl.ds(g * BLK, BLK), pl.ds(h * HD, HD)
        lin[rows, cols] = dot_nn(weights, v_ext[pl.ds(rim + g * BLK, BLK), cols]) + dot_nn(
            q_all[rows, cols], within[g, cols, :]
        )

    def window(g, earlier, with_intra):
        rows = pl.ds(g * BLK, BLK)
        for h in range(heads):
            cols = pl.ds(h * HD, HD)
            keys = pl.ds(g * BLK, (PREV + 1) * BLK)
            scores = dot_nt(q_all[rows, cols], k_ext[keys, cols])
            own = scores[:, PREV * BLK :]
            if with_intra:
                intra(g, own, h)
            seen = [scores[:, j * BLK : (j + 1) * BLK] + earlier[j] for j in range(PREV)]
            seen.append(jnp.where(causal, own + bias[pl.ds(g, 1), :], NEG))
            largest = functools.reduce(jnp.maximum, seen)
            largest = jnp.max(largest, axis=-1, keepdims=True)
            expd = [jnp.exp2((s - largest) * factor) for s in seen]
            denominator = jnp.sum(functools.reduce(jnp.add, expd), axis=-1, keepdims=True)
            inverse = 1.0 / denominator
            weights = jnp.concatenate([(e * inverse).astype(jnp.bfloat16) for e in expd], axis=1)
            local[rows, cols] = dot_nn(weights, v_ext[keys, cols])

    def switch(g, j):
        return jnp.where(mask_ref[PREV - 1 - j, g] == 1, 0.0, NEG)

    def inner_window(g):
        window(g, [bias[pl.ds(g - PREV + j, 1), :] + switch(g, j) for j in range(PREV)], True)

    @pl.when(relays)
    def _():
        for n, (source, target, relay) in enumerate(rims):
            push(n, source, relay, rim_send, hop_recv, ahead).wait_recv()
            push(n, relay, target, hop_send, rim_recv, head).start()

    @pl.loop(PREV, groups)
    def _(g):
        inner_window(g)

    def arrived(buffer, send, recv, count):
        return pltpu.make_async_remote_copy(
            src_ref=buffer.at[pl.ds(0, count)],
            dst_ref=buffer.at[pl.ds(0, count)],
            send_sem=send,
            recv_sem=recv,
            device_id={"inner": following},
            device_id_type=MESH,
        )

    @pl.loop(0, PREV)
    def _(g):
        for h in range(heads):
            cols = pl.ds(h * HD, HD)
            intra(
                g,
                dot_nt(q_all[pl.ds(g * BLK, BLK), cols], k_ext[pl.ds(rim + g * BLK, BLK), cols]),
                h,
            )

    def send_prefix(n):
        @pl.when(here != n)
        def _():
            pltpu.make_async_remote_copy(
                src_ref=prefixes.at[n],
                dst_ref=before.at[rank(here)],
                send_sem=prefix_send,
                recv_sem=prefix_recv,
                device_id={"inner": n},
                device_id_type=MESH,
            ).start()

    @pl.when(owner)
    def _():
        parts[pl.ds(here, 1)] = total[pl.ds(rank(here), 1)]
        so_far = jnp.zeros(parts.shape[1:], jnp.float32)
        for n in range(stages):
            members = stage - (n == stages - 1)
            mine = here // stage == n
            for own in range(2):
                if members > own:

                    @pl.when(mine if own else jnp.logical_not(mine))
                    def _(n=n, count=members - own):
                        arrived(parts, parts_send, parts_recv.at[n], count).wait_recv()

            following_spans = range(n * stage + 1, n * stage + members + 1)
            for m in following_spans:
                so_far = so_far + parts[m - 1].astype(jnp.float32)
                prefixes[m] = so_far.astype(jnp.bfloat16)
            early = [m for m in following_spans if n == 0 and m % line < half]
            for m in early:
                send_prefix(m)
            if n == 0:
                pl.semaphore_wait(ready, ni - owners)
            for m in following_spans:
                if m not in early:
                    send_prefix(m)

        @pl.when(jnp.logical_not(first))
        def _():
            before[pl.ds(rank(here), 1)] = prefixes[pl.ds(here, 1)]

    @pl.when(hub)
    def _():
        pl.semaphore_wait(entered, no - 1)
        for peer in outer_peers:
            pl.semaphore_signal(go, inc=1, device_id=peer, device_id_type=MESH)

    @pl.when(jnp.logical_and(owner, jnp.logical_not(first)))
    def _():
        arrived(before, prefix_send, prefix_recv, owners - 1).wait_recv()

    @pl.when(jnp.logical_not(owner))
    def _():
        arrived(before, prefix_send, prefix_recv, owners).wait_recv()


    carried = [
        before[pl.ds(h * each, each)].reshape(HD, HD) for h in range(heads)
    ]
    for g in range(groups):
        rows = pl.ds(g * BLK, BLK)
        powers = jnp.zeros((BLK, HD), jnp.float32)
        for h in range(heads):
            cols = pl.ds(h * HD, HD)
            whole = lin[rows, cols] + dot_nn(q_all[rows, cols], carried[h])
            lin[rows, cols] = whole
            powers = powers + whole * whole
        squares[pl.ds(g, 1), :] = jnp.sum(powers.T, axis=0, keepdims=True)

    all_squares[pl.ds(stripe, 1)] = squares[...][None]

    @pl.when(jnp.logical_not(hub))
    def _():
        pl.semaphore_wait(go, 1)


    for peer in outer_peers:
        pltpu.make_async_remote_copy(
            src_ref=squares,
            dst_ref=all_squares.at[stripe],
            send_sem=square_send,
            recv_sem=square_recv,
            device_id=peer,
            device_id_type=MESH,
        ).start()


    def rim_here(n):
        source, target, _ = rims[n]

        @pl.when(jnp.logical_not(first))
        def _():
            push(n, source, target, rim_send, rim_recv, following).wait_recv()

    rim_here(0)
    for g in reversed(range(PREV)):
        rim_here(2 * (PREV - g) - 1)
        rim_here(2 * (PREV - g))
        earlier = []
        for j in range(PREV):
            row = g - PREV + j
            source = rim_in if row < 0 else bias
            earlier.append(source[pl.ds(row % PREV if row < 0 else row, 1), :] + switch(g, j))
        window(g, earlier, False)

    arrived(all_squares, square_send, square_recv, no - 1).wait_recv()
    row_squares = jnp.sum(all_squares[...], axis=0)
    scale[...] = lax.rsqrt(row_squares / width + 1e-6)

    small[2].wait()
    stores = []
    for g in range(groups):
        rows = pl.ds(g * BLK, BLK)
        by_token = jnp.broadcast_to(scale[pl.ds(g, 1), :], (HD, BLK)).T
        for h in range(heads):
            cols = pl.ds(h * HD, HD)
            normed = lin[rows, cols] * by_token
            out[rows, cols] = (normed * gain_ref[:, cols] + local[rows, cols]).astype(jnp.bfloat16)
        stores.append(pltpu.make_async_copy(out.at[rows], o_hbm.at[rows], store_sem.at[g]))
        stores[-1].start()


    @pl.when(owner)
    def _():
        arrived(total, parts_send, parts_recv.at[0], owners - 1).wait_send()

        @pl.when(first)
        def _():
            arrived(prefixes, prefix_send, prefix_recv, ni - 1).wait_send()

        @pl.when(jnp.logical_not(first))
        def _():
            arrived(prefixes, prefix_send, prefix_recv, ni - 2).wait_send()

    @pl.when(jnp.logical_not(jnp.logical_or(owner, last)))
    def _():
        arrived(total, parts_send, parts_recv.at[0], owners).wait_send()

    arrived(all_squares, square_send, square_recv, no - 1).wait_send()

    @pl.when(jnp.logical_not(last))
    def _():
        for n, (source, target, _) in enumerate(rims):
            push(n, source, target, rim_send, rim_recv, following).wait_send()

    @pl.when(relays)
    def _():
        for n, (_, target, relay) in enumerate(rims):
            push(n, relay, target, hop_send, rim_recv, head).wait_send()

    for store in stores:
        store.wait()


def shards(ni, no, queries, keys, values, counts, window_mask, norm_gain):
    span, wide = queries.shape
    groups, heads = span // BLK, wide // HD
    owners = ni // 2
    piece = heads * HD // owners
    rim = PREV * BLK
    any_space = pl.BlockSpec(memory_space=pltpu.HBM)
    dma = pltpu.SemaphoreType.DMA
    f32, bf16 = jnp.float32, jnp.bfloat16
    return pl.pallas_call(
        functools.partial(kernel, ni, no, groups, heads),
        out_shape=jax.ShapeDtypeStruct((span, wide), bf16),
        in_specs=[any_space] * 6,
        out_specs=any_space,
        scratch_shapes=[
            pltpu.SMEM(counts.shape, jnp.int32),
            pltpu.SMEM(window_mask.shape[::-1], jnp.int32),
            pltpu.VMEM((1, wide), f32),
            pltpu.VMEM((span, wide), bf16),
            pltpu.VMEM((rim + span, wide), bf16),
            pltpu.VMEM((rim + span, wide), bf16),
            pltpu.VMEM((groups, heads * HD, HD), bf16),
            pltpu.VMEM((owners, piece, HD), bf16),
            pltpu.VMEM((ni, piece, HD), bf16),
            pltpu.VMEM((ni, piece, HD), bf16),
            pltpu.VMEM((owners, piece, HD), bf16),
            pltpu.VMEM((groups, BLK), f32),
            pltpu.VMEM((8, BLK), f32),
            pltpu.VMEM((8, BLK), f32),
            pltpu.VMEM((span, wide), f32),
            pltpu.VMEM((span, wide), f32),
            pltpu.VMEM((groups, BLK), f32),
            pltpu.VMEM((no, groups, BLK), f32),
            pltpu.VMEM((groups, BLK), f32),
            pltpu.VMEM((span, wide), bf16),
            dma((3,)),
            dma((2 * LOADS + 1,)),
            dma((groups,)),
            dma,
            dma((ni // max(1, ni // 8),)),
            dma,
            dma,
            dma((2 * PREV + 1,)),
            dma((2 * PREV + 1,)),
            dma,
            dma,
            pltpu.SemaphoreType.REGULAR,
            pltpu.SemaphoreType.REGULAR,
            pltpu.SemaphoreType.REGULAR,
            pltpu.VMEM((8, BLK), f32),
            pltpu.VMEM((rim, wide), bf16),
            pltpu.VMEM((rim, wide), bf16),
            dma((2 * PREV + 1,)),
            dma((2 * PREV + 1,)),
        ],
        compiler_params=pltpu.CompilerParams(
            collective_id=0, has_side_effects=True, vmem_limit_bytes=56 * 2**20
        ),
        name="layer",
    )(counts, window_mask.T, norm_gain.reshape(1, wide), queries, keys, values)


def solution(mesh):
    return jax.shard_map(
        functools.partial(shards, mesh.shape["inner"], mesh.shape["outer"]),
        mesh=mesh,
        in_specs=(
            P("inner", "outer"),
            P("inner", "outer"),
            P("inner", "outer"),
            P("inner"),
            P("inner", None),
            P("outer"),
        ),
        out_specs=P("inner", "outer"),
        check_vma=False,
    )
```

```python
import functools

import jax
import jax.numpy as jnp
from jax import lax
from jax.experimental import pallas as pl
from jax.experimental.pallas import tpu as pltpu
from jax.sharding import PartitionSpec as P

HD = 128
BLK = 128
PREV = 3
LOADS = 4
MESH = pl.DeviceIdType.MESH
NEG = -1e30
LOG2E = 1.4426950408889634


def far_first(size):
    return sorted(range(size), key=lambda s: min(s, size - s), reverse=True)


def dot_nt(a, b):
    return lax.dot_general(a, b, (((1,), (1,)), ((), ())), preferred_element_type=jnp.float32)


def dot_tn(a, b):
    return lax.dot_general(a, b, (((0,), (0,)), ((), ())), preferred_element_type=jnp.float32)


def dot_nn(a, b):
    return lax.dot_general(a, b, (((1,), (0,)), ((), ())), preferred_element_type=jnp.float32)


def kernel(
    ni,
    no,
    groups,
    heads,
    counts_hbm,
    mask_hbm,
    gain_hbm,
    q_hbm,
    k_hbm,
    v_hbm,
    out,
    counts_ref,
    mask_ref,
    gain_ref,
    q_all,
    k_ext,
    v_ext,
    within,
    total,
    parts,
    prefixes,
    before,
    bias,
    rim_out,
    rim_in,
    lin,
    local,
    squares,
    all_squares,
    scale,
    small_sem,
    load_sem,
    parts_send,
    parts_recv,
    prefix_send,
    prefix_recv,
    rim_send,
    rim_recv,
    square_send,
    square_recv,
    ready,
    entered,
    go,
    relay_bias,
    relay_keys,
    relay_values,
    hop_send,
    hop_recv,
):
    rim = PREV * BLK
    span = groups * BLK
    width = no * heads * HD
    here = lax.axis_index("inner")
    stripe = lax.axis_index("outer")
    following = lax.rem(here + 1, ni)

    small = [
        pltpu.make_async_copy(counts_hbm, counts_ref, small_sem.at[0]),
        pltpu.make_async_copy(mask_hbm, mask_ref, small_sem.at[1]),
        pltpu.make_async_copy(gain_hbm, gain_ref, small_sem.at[2]),
    ]
    chunk = span // LOADS
    loads = []
    for n in range(LOADS):
        rows, ext = pl.ds(n * chunk, chunk), pl.ds(rim + n * chunk, chunk)
        loads.append(pltpu.make_async_copy(k_hbm.at[rows], k_ext.at[ext], load_sem.at[2 * n]))
        loads.append(pltpu.make_async_copy(v_hbm.at[rows], v_ext.at[ext], load_sem.at[2 * n + 1]))
    load_q = pltpu.make_async_copy(q_hbm, q_all, load_sem.at[2 * LOADS])
    small[0].start()
    for load in loads:
        load.start()
    small[1].start()
    small[2].start()
    load_q.start()

    barrier = pltpu.get_barrier_semaphore()
    inner_sizes = {32: (4, 8), 8: (2, 4)}.get(ni, (1, ni))
    outer_sizes = (8, 2) if no == 16 else (no, 1)
    rows_of_chips, line = inner_sizes
    layers, cores = outer_sizes
    half = line // 2
    owners = ni // 2

    def owns(place):
        return lax.rem(place, line) < half

    def rank(place):
        return lax.div(place, line) * half + lax.rem(place, line)

    owner = owns(here)
    preceding = lax.rem(here + ni - 1, ni)
    first, last = here == 0, here == ni - 1
    tail = lax.rem(here, line) == line - 1
    straight = jnp.logical_not(tail)
    detour = jnp.logical_and(tail, jnp.logical_not(last))
    relays = jnp.logical_and(tail, here >= line)
    ahead = lax.rem(here + line, ni)
    behind = lax.rem(here + ni - line, ni)
    along, across = lax.rem(here, line), lax.div(here, line)
    head = across * line
    rows_far_first = [
        (dx, lax.rem(across + dx, rows_of_chips) * line) for dx in far_first(rows_of_chips)
    ]
    tall, deep = lax.div(stripe, cores), lax.rem(stripe, cores)

    def to_outer(act):
        for dy in far_first(layers):
            base = lax.rem(tall + dy, layers) * cores
            for dc in range(cores):
                if dy or dc:
                    act({"outer": base + lax.rem(deep + dc, cores)})

    def to_inner(act, only_owners):
        for dz in far_first(line):
            z = lax.rem(along + dz, line)

            def send(dz=dz, z=z):
                for dx, row in rows_far_first:
                    if dx or dz:
                        act(row + z, lax.div(row, 2) + z)

            if only_owners:
                pl.when(z < half)(send)
            else:
                send()

    def greet(peer):
        pl.semaphore_signal(barrier, inc=1, device_id=peer, device_id_type=MESH)

    @pl.when(owner)
    def _():
        to_inner(lambda there, _: greet({"inner": there}), False)

    @pl.when(jnp.logical_not(owner))
    def _():
        pl.semaphore_signal(barrier, inc=1, device_id={"inner": preceding}, device_id_type=MESH)

    @pl.when(relays)
    def _():
        pl.semaphore_signal(barrier, inc=1, device_id={"inner": behind}, device_id_type=MESH)

    hub = stripe == 0

    @pl.when(hub)
    def _():
        to_outer(greet)

    small[0].wait()
    lane = lax.broadcasted_iota(jnp.int32, (1, BLK), 1)
    for g in range(groups):
        bias[pl.ds(g, 1), :] = jnp.where(lane < counts_ref[g], 0.0, NEG)
    rim_out[...] = jnp.full(rim_out.shape, NEG, jnp.float32)
    for j in range(PREV):
        rim_out[pl.ds(j, 1), :] = bias[pl.ds(groups - PREV + j, 1), :]

    greeters = (
        owners
        - jnp.where(owner, 1, 0)
        + jnp.where(owns(following), 0, 1)
        + jnp.where(detour, 1, 0)
        + jnp.where(hub, 0, 1)
    )
    rims = [(rim_out, rim_in, relay_bias)]
    for n in reversed(range(PREV)):
        for ext, relay in ((k_ext, relay_keys), (v_ext, relay_values)):
            near, far = pl.ds(n * BLK, BLK), pl.ds(span + n * BLK, BLK)
            rims.append((ext.at[far], ext.at[near], relay.at[near]))

    def push(n, source, target, send, recv, there):
        return pltpu.make_async_remote_copy(
            src_ref=source,
            dst_ref=target,
            send_sem=send.at[n],
            recv_sem=recv.at[n],
            device_id={"inner": there},
            device_id_type=MESH,
        )

    token = lax.broadcasted_iota(jnp.int32, (BLK, HD), 0)
    each = owners // heads
    piece = heads * HD // owners
    running = [jnp.zeros((HD, HD), jnp.float32)] * heads
    for g in range(groups):
        if (g * BLK) % chunk == 0:
            loads[2 * (g * BLK // chunk)].wait()
            loads[2 * (g * BLK // chunk) + 1].wait()
        for h in range(heads):
            cols = pl.ds(h * HD, HD)
            rows = pl.ds(rim + g * BLK, BLK)
            masked = jnp.where(token < counts_ref[g], k_ext[rows, cols], jnp.zeros((), jnp.bfloat16))
            if g:
                within[g, cols, :] = running[h].astype(jnp.bfloat16)
            running[h] = running[h] + dot_tn(masked, v_ext[rows, cols])
    for h in range(heads):
        total[pl.ds(h * each, each)] = running[h].reshape(each, piece, HD).astype(jnp.bfloat16)
    within[0] = jnp.zeros(within.shape[1:], jnp.bfloat16)

    pl.semaphore_wait(barrier, greeters)

    stage = max(1, ni // 8)
    stages = ni // stage
    my_stage = lax.div(here, stage)

    def send_part(there, place):
        pltpu.make_async_remote_copy(
            src_ref=total.at[place],
            dst_ref=parts.at[here],
            send_sem=parts_send,
            recv_sem=parts_recv.at[my_stage],
            device_id={"inner": there},
            device_id_type=MESH,
        ).start()

    @pl.when(jnp.logical_not(last))
    def _():
        to_inner(send_part, True)

    @pl.when(detour)
    def _():
        for n, (source, _, relay) in enumerate(rims):
            push(n, source, relay, rim_send, hop_recv, ahead).start()

    @pl.when(straight)
    def _():
        for n, (source, target, _) in enumerate(rims):
            push(n, source, target, rim_send, rim_recv, following).start()

    @pl.when(first)
    def _():
        rim_in[...] = jnp.full(rim_in.shape, NEG, jnp.float32)
        before[...] = jnp.zeros(before.shape, jnp.bfloat16)
        k_ext[pl.ds(0, rim)] = jnp.zeros((rim, k_ext.shape[1]), jnp.bfloat16)
        v_ext[pl.ds(0, rim)] = jnp.zeros((rim, v_ext.shape[1]), jnp.bfloat16)

    @pl.when(jnp.logical_not(hub))
    def _():
        pl.semaphore_signal(entered, inc=1, device_id={"outer": 0}, device_id_type=MESH)

    @pl.when(jnp.logical_not(owner))
    def _():
        for n in range(owners):
            pl.semaphore_signal(
                ready,
                inc=1,
                device_id={"inner": n // half * line + n % half},
                device_id_type=MESH,
            )

    load_q.wait()
    small[1].wait()
    causal = lax.broadcasted_iota(jnp.int32, (BLK, BLK), 0) >= lax.broadcasted_iota(
        jnp.int32, (BLK, BLK), 1
    )
    factor = LOG2E / HD**0.5

    def intra(g, scores, h):
        valid = causal & (bias[pl.ds(g, 1), :] == 0.0)
        weights = jnp.where(valid, scores, 0.0).astype(jnp.bfloat16)
        rows, cols = pl.ds(g * BLK, BLK), pl.ds(h * HD, HD)
        lin[rows, cols] = dot_nn(weights, v_ext[pl.ds(rim + g * BLK, BLK), cols]) + dot_nn(
            q_all[rows, cols], within[g, cols, :]
        )

    def window(g, earlier, with_intra):
        rows = pl.ds(g * BLK, BLK)
        for h in range(heads):
            cols = pl.ds(h * HD, HD)
            keys = pl.ds(g * BLK, (PREV + 1) * BLK)
            scores = dot_nt(q_all[rows, cols], k_ext[keys, cols])
            own = scores[:, PREV * BLK :]
            if with_intra:
                intra(g, own, h)
            seen = [scores[:, j * BLK : (j + 1) * BLK] + earlier[j] for j in range(PREV)]
            seen.append(jnp.where(causal, own + bias[pl.ds(g, 1), :], NEG))
            largest = functools.reduce(jnp.maximum, seen)
            largest = jnp.max(largest, axis=-1, keepdims=True)
            expd = [jnp.exp2((s - largest) * factor) for s in seen]
            denominator = jnp.sum(functools.reduce(jnp.add, expd), axis=-1, keepdims=True)
            inverse = 1.0 / denominator
            weights = jnp.concatenate([(e * inverse).astype(jnp.bfloat16) for e in expd], axis=1)
            local[rows, cols] = dot_nn(weights, v_ext[keys, cols])

    def switch(g, j):
        return jnp.where(mask_ref[PREV - 1 - j, g] == 1, 0.0, NEG)

    def inner_window(g):
        window(g, [bias[pl.ds(g - PREV + j, 1), :] + switch(g, j) for j in range(PREV)], True)

    @pl.when(relays)
    def _():
        for n, (source, target, relay) in enumerate(rims):
            push(n, source, relay, rim_send, hop_recv, ahead).wait_recv()
            push(n, relay, target, hop_send, rim_recv, head).start()

    @pl.loop(PREV, groups)
    def _(g):
        inner_window(g)

    def arrived(buffer, send, recv, count):
        return pltpu.make_async_remote_copy(
            src_ref=buffer.at[pl.ds(0, count)],
            dst_ref=buffer.at[pl.ds(0, count)],
            send_sem=send,
            recv_sem=recv,
            device_id={"inner": following},
            device_id_type=MESH,
        )

    @pl.loop(0, PREV)
    def _(g):
        for h in range(heads):
            cols = pl.ds(h * HD, HD)
            intra(
                g,
                dot_nt(q_all[pl.ds(g * BLK, BLK), cols], k_ext[pl.ds(rim + g * BLK, BLK), cols]),
                h,
            )

    def send_prefix(n):
        @pl.when(here != n)
        def _():
            pltpu.make_async_remote_copy(
                src_ref=prefixes.at[n],
                dst_ref=before.at[rank(here)],
                send_sem=prefix_send,
                recv_sem=prefix_recv,
                device_id={"inner": n},
                device_id_type=MESH,
            ).start()

    @pl.when(owner)
    def _():
        parts[pl.ds(here, 1)] = total[pl.ds(rank(here), 1)]
        so_far = jnp.zeros(parts.shape[1:], jnp.float32)
        held = []
        for n in range(stages):
            members = stage - (n == stages - 1)
            mine = my_stage == n
            for own in range(2):
                if members > own:

                    @pl.when(mine if own else jnp.logical_not(mine))
                    def _(n=n, count=members - own):
                        arrived(parts, parts_send, parts_recv.at[n], count).wait_recv()

            following_spans = range(n * stage + 1, n * stage + members + 1)
            for m in following_spans:
                so_far = so_far + parts[m - 1].astype(jnp.float32)
                prefixes[m] = so_far.astype(jnp.bfloat16)
            for m in following_spans:
                if m % line < half:
                    send_prefix(m)
            held += [m for m in following_spans if m % line >= half]
            if n == stages - 1:
                pl.semaphore_wait(ready, ni - owners)
                for m in held:
                    send_prefix(m)

        @pl.when(jnp.logical_not(first))
        def _():
            before[pl.ds(rank(here), 1)] = prefixes[pl.ds(here, 1)]

    @pl.when(hub)
    def _():
        pl.semaphore_wait(entered, no - 1)
        to_outer(
            lambda peer: pl.semaphore_signal(go, inc=1, device_id=peer, device_id_type=MESH)
        )

    @pl.when(jnp.logical_and(owner, jnp.logical_not(first)))
    def _():
        arrived(before, prefix_send, prefix_recv, owners - 1).wait_recv()

    @pl.when(jnp.logical_not(owner))
    def _():
        arrived(before, prefix_send, prefix_recv, owners).wait_recv()


    carried = [
        before[pl.ds(h * each, each)].reshape(HD, HD) for h in range(heads)
    ]
    for g in range(groups):
        rows = pl.ds(g * BLK, BLK)
        powers = jnp.zeros((BLK, HD), jnp.float32)
        for h in range(heads):
            cols = pl.ds(h * HD, HD)
            whole = lin[rows, cols] + dot_nn(q_all[rows, cols], carried[h])
            lin[rows, cols] = whole
            powers = powers + whole * whole
        squares[pl.ds(g, 1), :] = jnp.sum(powers.T, axis=0, keepdims=True)

    all_squares[pl.ds(stripe, 1)] = squares[...][None]

    @pl.when(jnp.logical_not(hub))
    def _():
        pl.semaphore_wait(go, 1)


    to_outer(
        lambda peer: pltpu.make_async_remote_copy(
            src_ref=squares,
            dst_ref=all_squares.at[stripe],
            send_sem=square_send,
            recv_sem=square_recv,
            device_id=peer,
            device_id_type=MESH,
        ).start()
    )

    def rim_here(n):
        source, target, _ = rims[n]

        @pl.when(jnp.logical_not(first))
        def _():
            push(n, source, target, rim_send, rim_recv, following).wait_recv()

    rim_here(0)
    for g in reversed(range(PREV)):
        rim_here(2 * (PREV - g) - 1)
        rim_here(2 * (PREV - g))
        earlier = []
        for j in range(PREV):
            row = g - PREV + j
            source = rim_in if row < 0 else bias
            earlier.append(source[pl.ds(row % PREV if row < 0 else row, 1), :] + switch(g, j))
        window(g, earlier, False)

    arrived(all_squares, square_send, square_recv, no - 1).wait_recv()
    row_squares = jnp.sum(all_squares[...], axis=0)
    scale[...] = lax.rsqrt(row_squares / width + 1e-6)

    small[2].wait()
    for g in range(groups):
        rows = pl.ds(g * BLK, BLK)
        by_token = jnp.broadcast_to(scale[pl.ds(g, 1), :], (HD, BLK)).T
        for h in range(heads):
            cols = pl.ds(h * HD, HD)
            normed = lin[rows, cols] * by_token
            out[rows, cols] = (normed * gain_ref[:, cols] + local[rows, cols]).astype(jnp.bfloat16)


    @pl.when(owner)
    def _():
        arrived(total, parts_send, parts_recv.at[0], owners - 1).wait_send()

        @pl.when(first)
        def _():
            arrived(prefixes, prefix_send, prefix_recv, ni - 1).wait_send()

        @pl.when(jnp.logical_not(first))
        def _():
            arrived(prefixes, prefix_send, prefix_recv, ni - 2).wait_send()

    @pl.when(jnp.logical_not(jnp.logical_or(owner, last)))
    def _():
        arrived(total, parts_send, parts_recv.at[0], owners).wait_send()

    arrived(all_squares, square_send, square_recv, no - 1).wait_send()

    @pl.when(jnp.logical_not(last))
    def _():
        for n, (source, target, _) in enumerate(rims):
            push(n, source, target, rim_send, rim_recv, following).wait_send()

    @pl.when(relays)
    def _():
        for n, (_, target, relay) in enumerate(rims):
            push(n, relay, target, hop_send, rim_recv, head).wait_send()


def shards(ni, no, queries, keys, values, counts, window_mask, norm_gain):
    span, wide = queries.shape
    groups, heads = span // BLK, wide // HD
    owners = ni // 2
    piece = heads * HD // owners
    rim = PREV * BLK
    any_space = pl.BlockSpec(memory_space=pltpu.HBM)
    dma = pltpu.SemaphoreType.DMA
    f32, bf16 = jnp.float32, jnp.bfloat16
    return pl.pallas_call(
        functools.partial(kernel, ni, no, groups, heads),
        out_shape=jax.ShapeDtypeStruct((span, wide), bf16),
        in_specs=[any_space] * 6,
        out_specs=pl.BlockSpec(memory_space=pltpu.VMEM),
        scratch_shapes=[
            pltpu.SMEM(counts.shape, jnp.int32),
            pltpu.SMEM(window_mask.shape[::-1], jnp.int32),
            pltpu.VMEM((1, wide), f32),
            pltpu.VMEM((span, wide), bf16),
            pltpu.VMEM((rim + span, wide), bf16),
            pltpu.VMEM((rim + span, wide), bf16),
            pltpu.VMEM((groups, heads * HD, HD), bf16),
            pltpu.VMEM((owners, piece, HD), bf16),
            pltpu.VMEM((ni, piece, HD), bf16),
            pltpu.VMEM((ni, piece, HD), bf16),
            pltpu.VMEM((owners, piece, HD), bf16),
            pltpu.VMEM((groups, BLK), f32),
            pltpu.VMEM((8, BLK), f32),
            pltpu.VMEM((8, BLK), f32),
            pltpu.VMEM((span, wide), f32),
            pltpu.VMEM((span, wide), f32),
            pltpu.VMEM((groups, BLK), f32),
            pltpu.VMEM((no, groups, BLK), f32),
            pltpu.VMEM((groups, BLK), f32),
            dma((3,)),
            dma((2 * LOADS + 1,)),
            dma,
            dma((ni // max(1, ni // 8),)),
            dma,
            dma,
            dma((2 * PREV + 1,)),
            dma((2 * PREV + 1,)),
            dma,
            dma,
            pltpu.SemaphoreType.REGULAR,
            pltpu.SemaphoreType.REGULAR,
            pltpu.SemaphoreType.REGULAR,
            pltpu.VMEM((8, BLK), f32),
            pltpu.VMEM((rim, wide), bf16),
            pltpu.VMEM((rim, wide), bf16),
            dma((2 * PREV + 1,)),
            dma((2 * PREV + 1,)),
        ],
        compiler_params=pltpu.CompilerParams(
            collective_id=0, has_side_effects=True, vmem_limit_bytes=40 * 2**20
        ),
        name="layer",
    )(*(pltpu.with_memory_space_constraint(x, pltpu.HBM) for x in (counts, window_mask.T, norm_gain.reshape(1, wide), queries, keys, values)))


def solution(mesh):
    return jax.shard_map(
        functools.partial(shards, mesh.shape["inner"], mesh.shape["outer"]),
        mesh=mesh,
        in_specs=(
            P("inner", "outer"),
            P("inner", "outer"),
            P("inner", "outer"),
            P("inner"),
            P("inner", None),
            P("outer"),
        ),
        out_specs=P("inner", "outer"),
        check_vma=False,
    )
```

```python
import functools

import jax
import jax.numpy as jnp
from jax import lax
from jax.experimental import pallas as pl
from jax.experimental.pallas import tpu as pltpu
from jax.sharding import PartitionSpec as P

HD = 128
BLK = 128
PREV = 3
LOADS = 4
MESH = pl.DeviceIdType.MESH
NEG = -1e30
LOG2E = 1.4426950408889634


def far_first(size):
    return sorted(range(size), key=lambda s: min(s, size - s), reverse=True)


def dot_nt(a, b):
    return lax.dot_general(a, b, (((1,), (1,)), ((), ())), preferred_element_type=jnp.float32)


def dot_tn(a, b):
    return lax.dot_general(a, b, (((0,), (0,)), ((), ())), preferred_element_type=jnp.float32)


def dot_nn(a, b):
    return lax.dot_general(a, b, (((1,), (0,)), ((), ())), preferred_element_type=jnp.float32)


def kernel(
    ni,
    no,
    groups,
    heads,
    counts_hbm,
    mask_hbm,
    gain_hbm,
    q_hbm,
    k_hbm,
    v_hbm,
    out,
    counts_ref,
    mask_ref,
    gain_ref,
    q_all,
    k_ext,
    v_ext,
    within,
    total,
    parts,
    prefixes,
    before,
    bias,
    rim_out,
    rim_in,
    lin,
    local,
    squares,
    all_squares,
    scale,
    small_sem,
    load_sem,
    parts_send,
    parts_recv,
    prefix_send,
    prefix_recv,
    rim_send,
    rim_recv,
    square_send,
    square_recv,
    ready,
    entered,
    go,
    relay_bias,
    relay_keys,
    relay_values,
    hop_send,
    hop_recv,
):
    rim = PREV * BLK
    span = groups * BLK
    width = no * heads * HD
    here = lax.axis_index("inner")
    stripe = lax.axis_index("outer")
    following = lax.rem(here + 1, ni)

    small = [
        pltpu.make_async_copy(counts_hbm, counts_ref, small_sem.at[0]),
        pltpu.make_async_copy(mask_hbm, mask_ref, small_sem.at[1]),
        pltpu.make_async_copy(gain_hbm, gain_ref, small_sem.at[2]),
    ]
    chunk = span // LOADS
    loads = []
    for n in range(LOADS):
        rows, ext = pl.ds(n * chunk, chunk), pl.ds(rim + n * chunk, chunk)
        loads.append(pltpu.make_async_copy(k_hbm.at[rows], k_ext.at[ext], load_sem.at[2 * n]))
        loads.append(pltpu.make_async_copy(v_hbm.at[rows], v_ext.at[ext], load_sem.at[2 * n + 1]))
    load_q = pltpu.make_async_copy(q_hbm, q_all, load_sem.at[2 * LOADS])
    small[0].start()
    for load in loads:
        load.start()
    small[1].start()
    small[2].start()
    load_q.start()

    barrier = pltpu.get_barrier_semaphore()
    inner_sizes = {32: (4, 8), 8: (2, 4)}.get(ni, (1, ni))
    outer_sizes = (8, 2) if no == 16 else (no, 1)
    rows_of_chips, line = inner_sizes
    layers, cores = outer_sizes
    half = line // 2
    owners = ni // 2

    def owns(place):
        return lax.rem(place, line) < half

    def rank(place):
        return lax.div(place, line) * half + lax.rem(place, line)

    owner = owns(here)
    preceding = lax.rem(here + ni - 1, ni)
    first, last = here == 0, here == ni - 1
    tail = lax.rem(here, line) == line - 1
    straight = jnp.logical_not(tail)
    detour = jnp.logical_and(tail, jnp.logical_not(last))
    relays = jnp.logical_and(tail, here >= line)
    ahead = lax.rem(here + line, ni)
    behind = lax.rem(here + ni - line, ni)
    along, across = lax.rem(here, line), lax.div(here, line)
    head = across * line
    rows_far_first = [
        (dx, lax.rem(across + dx, rows_of_chips) * line) for dx in far_first(rows_of_chips)
    ]
    tall, deep = lax.div(stripe, cores), lax.rem(stripe, cores)

    def to_outer(act):
        for dy in far_first(layers):
            base = lax.rem(tall + dy, layers) * cores
            for dc in range(cores):
                if dy or dc:
                    act({"outer": base + lax.rem(deep + dc, cores)})

    def to_inner(act, only_owners):
        for dz in far_first(line):
            z = lax.rem(along + dz, line)

            def send(dz=dz, z=z):
                for dx, row in rows_far_first:
                    if dx or dz:
                        act(row + z, lax.div(row, 2) + z)

            if only_owners:
                pl.when(z < half)(send)
            else:
                send()

    def greet(peer):
        pl.semaphore_signal(barrier, inc=1, device_id=peer, device_id_type=MESH)

    @pl.when(owner)
    def _():
        to_inner(lambda there, _: greet({"inner": there}), False)

    @pl.when(jnp.logical_not(owner))
    def _():
        pl.semaphore_signal(barrier, inc=1, device_id={"inner": preceding}, device_id_type=MESH)

    @pl.when(relays)
    def _():
        pl.semaphore_signal(barrier, inc=1, device_id={"inner": behind}, device_id_type=MESH)

    hub = stripe == 0

    @pl.when(hub)
    def _():
        to_outer(greet)

    small[0].wait()
    lane = lax.broadcasted_iota(jnp.int32, (1, BLK), 1)
    for g in range(groups):
        bias[pl.ds(g, 1), :] = jnp.where(lane < counts_ref[g], 0.0, NEG)
    rim_out[...] = jnp.full(rim_out.shape, NEG, jnp.float32)
    for j in range(PREV):
        rim_out[pl.ds(j, 1), :] = bias[pl.ds(groups - PREV + j, 1), :]

    greeters = (
        owners
        - jnp.where(owner, 1, 0)
        + jnp.where(owns(following), 0, 1)
        + jnp.where(detour, 1, 0)
        + jnp.where(hub, 0, 1)
    )
    rims = [(rim_out, rim_in, relay_bias)]
    for n in reversed(range(PREV)):
        for ext, relay in ((k_ext, relay_keys), (v_ext, relay_values)):
            near, far = pl.ds(n * BLK, BLK), pl.ds(span + n * BLK, BLK)
            rims.append((ext.at[far], ext.at[near], relay.at[near]))

    def push(n, source, target, send, recv, there):
        return pltpu.make_async_remote_copy(
            src_ref=source,
            dst_ref=target,
            send_sem=send.at[n],
            recv_sem=recv.at[n],
            device_id={"inner": there},
            device_id_type=MESH,
        )

    token = lax.broadcasted_iota(jnp.int32, (BLK, HD), 0)
    each = owners // heads
    piece = heads * HD // owners
    running = [jnp.zeros((HD, HD), jnp.float32)] * heads
    for g in range(groups):
        if (g * BLK) % chunk == 0:
            loads[2 * (g * BLK // chunk)].wait()
            loads[2 * (g * BLK // chunk) + 1].wait()
        for h in range(heads):
            cols = pl.ds(h * HD, HD)
            rows = pl.ds(rim + g * BLK, BLK)
            masked = jnp.where(token < counts_ref[g], k_ext[rows, cols], jnp.zeros((), jnp.bfloat16))
            if g:
                within[g, cols, :] = running[h].astype(jnp.bfloat16)
            running[h] = running[h] + dot_tn(masked, v_ext[rows, cols])
    for h in range(heads):
        total[pl.ds(h * each, each)] = running[h].reshape(each, piece, HD).astype(jnp.bfloat16)
    within[0] = jnp.zeros(within.shape[1:], jnp.bfloat16)

    pl.semaphore_wait(barrier, greeters)

    stage = max(1, ni // 8)
    stages = ni // stage
    my_stage = lax.div(here, stage)

    def send_part(there, place):
        pltpu.make_async_remote_copy(
            src_ref=total.at[place],
            dst_ref=parts.at[here],
            send_sem=parts_send,
            recv_sem=parts_recv.at[my_stage],
            device_id={"inner": there},
            device_id_type=MESH,
        ).start()

    @pl.when(jnp.logical_not(last))
    def _():
        to_inner(send_part, True)

    @pl.when(detour)
    def _():
        for n, (source, _, relay) in enumerate(rims):
            push(n, source, relay, rim_send, hop_recv, ahead).start()

    @pl.when(straight)
    def _():
        for n, (source, target, _) in enumerate(rims):
            push(n, source, target, rim_send, rim_recv, following).start()

    @pl.when(first)
    def _():
        rim_in[...] = jnp.full(rim_in.shape, NEG, jnp.float32)
        before[...] = jnp.zeros(before.shape, jnp.bfloat16)
        k_ext[pl.ds(0, rim)] = jnp.zeros((rim, k_ext.shape[1]), jnp.bfloat16)
        v_ext[pl.ds(0, rim)] = jnp.zeros((rim, v_ext.shape[1]), jnp.bfloat16)

    @pl.when(jnp.logical_not(hub))
    def _():
        pl.semaphore_signal(entered, inc=1, device_id={"outer": 0}, device_id_type=MESH)

    @pl.when(jnp.logical_not(owner))
    def _():
        for n in range(owners):
            pl.semaphore_signal(
                ready,
                inc=1,
                device_id={"inner": n // half * line + n % half},
                device_id_type=MESH,
            )

    load_q.wait()
    small[1].wait()
    causal = lax.broadcasted_iota(jnp.int32, (BLK, BLK), 0) >= lax.broadcasted_iota(
        jnp.int32, (BLK, BLK), 1
    )
    factor = LOG2E / HD**0.5

    def intra(g, scores, h):
        valid = causal & (bias[pl.ds(g, 1), :] == 0.0)
        weights = jnp.where(valid, scores, 0.0).astype(jnp.bfloat16)
        rows, cols = pl.ds(g * BLK, BLK), pl.ds(h * HD, HD)
        lin[rows, cols] = dot_nn(weights, v_ext[pl.ds(rim + g * BLK, BLK), cols]) + dot_nn(
            q_all[rows, cols], within[g, cols, :]
        )

    def window(g, earlier, with_intra):
        rows = pl.ds(g * BLK, BLK)
        for h in range(heads):
            cols = pl.ds(h * HD, HD)
            keys = pl.ds(g * BLK, (PREV + 1) * BLK)
            scores = dot_nt(q_all[rows, cols], k_ext[keys, cols])
            own = scores[:, PREV * BLK :]
            if with_intra:
                intra(g, own, h)
            seen = [scores[:, j * BLK : (j + 1) * BLK] + earlier[j] for j in range(PREV)]
            seen.append(jnp.where(causal, own + bias[pl.ds(g, 1), :], NEG))
            largest = functools.reduce(jnp.maximum, seen)
            largest = jnp.max(largest, axis=-1, keepdims=True)
            expd = [jnp.exp2((s - largest) * factor) for s in seen]
            denominator = jnp.sum(functools.reduce(jnp.add, expd), axis=-1, keepdims=True)
            inverse = 1.0 / denominator
            weights = jnp.concatenate([(e * inverse).astype(jnp.bfloat16) for e in expd], axis=1)
            local[rows, cols] = dot_nn(weights, v_ext[keys, cols])

    def switch(g, j):
        return jnp.where(mask_ref[PREV - 1 - j, g] == 1, 0.0, NEG)

    def inner_window(g):
        window(g, [bias[pl.ds(g - PREV + j, 1), :] + switch(g, j) for j in range(PREV)], True)

    @pl.when(relays)
    def _():
        for n, (source, target, relay) in enumerate(rims):
            push(n, source, relay, rim_send, hop_recv, ahead).wait_recv()
            push(n, relay, target, hop_send, rim_recv, head).start()

    @pl.loop(PREV, groups)
    def _(g):
        inner_window(g)

    def arrived(buffer, send, recv, count):
        return pltpu.make_async_remote_copy(
            src_ref=buffer.at[pl.ds(0, count)],
            dst_ref=buffer.at[pl.ds(0, count)],
            send_sem=send,
            recv_sem=recv,
            device_id={"inner": following},
            device_id_type=MESH,
        )

    @pl.loop(0, PREV)
    def _(g):
        for h in range(heads):
            cols = pl.ds(h * HD, HD)
            intra(
                g,
                dot_nt(q_all[pl.ds(g * BLK, BLK), cols], k_ext[pl.ds(rim + g * BLK, BLK), cols]),
                h,
            )

    def send_prefix(n):
        @pl.when(here != n)
        def _():
            pltpu.make_async_remote_copy(
                src_ref=prefixes.at[n],
                dst_ref=before.at[rank(here)],
                send_sem=prefix_send,
                recv_sem=prefix_recv,
                device_id={"inner": n},
                device_id_type=MESH,
            ).start()

    @pl.when(owner)
    def _():
        parts[pl.ds(here, 1)] = total[pl.ds(rank(here), 1)]
        so_far = jnp.zeros(parts.shape[1:], jnp.float32)
        held = []
        for n in range(stages):
            members = stage - (n == stages - 1)
            mine = my_stage == n
            for own in range(2):
                if members > own:

                    @pl.when(mine if own else jnp.logical_not(mine))
                    def _(n=n, count=members - own):
                        arrived(parts, parts_send, parts_recv.at[n], count).wait_recv()

            following_spans = range(n * stage + 1, n * stage + members + 1)
            for m in following_spans:
                so_far = so_far + parts[m - 1].astype(jnp.float32)
                prefixes[m] = so_far.astype(jnp.bfloat16)
            for m in following_spans:
                if m % line < half:
                    send_prefix(m)
            held += [m for m in following_spans if m % line >= half]
            if n == stages - 1:
                pl.semaphore_wait(ready, ni - owners)
                for m in held:
                    send_prefix(m)

        @pl.when(jnp.logical_not(first))
        def _():
            before[pl.ds(rank(here), 1)] = prefixes[pl.ds(here, 1)]

    @pl.when(hub)
    def _():
        pl.semaphore_wait(entered, no - 1)
        to_outer(
            lambda peer: pl.semaphore_signal(go, inc=1, device_id=peer, device_id_type=MESH)
        )

    @pl.when(jnp.logical_and(owner, jnp.logical_not(first)))
    def _():
        arrived(before, prefix_send, prefix_recv, owners - 1).wait_recv()

    @pl.when(jnp.logical_not(owner))
    def _():
        arrived(before, prefix_send, prefix_recv, owners).wait_recv()


    blank = jnp.zeros((HD, HD), jnp.bfloat16)
    carried = jnp.concatenate(
        [
            jnp.concatenate(
                [
                    before[pl.ds(h * each, each)].reshape(HD, HD) if h == n else blank
                    for n in range(heads)
                ],
                axis=1,
            )
            for h in range(heads)
        ],
        axis=0,
    )
    for g in range(groups):
        rows = pl.ds(g * BLK, BLK)
        whole = lin[rows, :] + dot_nn(q_all[rows, :], carried)
        lin[rows, :] = whole
        powers = whole * whole
        powers = sum(powers[:, h * HD : (h + 1) * HD] for h in range(heads))
        squares[pl.ds(g, 1), :] = jnp.sum(powers.T, axis=0, keepdims=True)

    all_squares[pl.ds(stripe, 1)] = squares[...][None]

    @pl.when(jnp.logical_not(hub))
    def _():
        pl.semaphore_wait(go, 1)


    to_outer(
        lambda peer: pltpu.make_async_remote_copy(
            src_ref=squares,
            dst_ref=all_squares.at[stripe],
            send_sem=square_send,
            recv_sem=square_recv,
            device_id=peer,
            device_id_type=MESH,
        ).start()
    )

    def rim_here(n):
        source, target, _ = rims[n]

        @pl.when(jnp.logical_not(first))
        def _():
            push(n, source, target, rim_send, rim_recv, following).wait_recv()

    rim_here(0)
    for g in reversed(range(PREV)):
        rim_here(2 * (PREV - g) - 1)
        rim_here(2 * (PREV - g))
        earlier = []
        for j in range(PREV):
            row = g - PREV + j
            source = rim_in if row < 0 else bias
            earlier.append(source[pl.ds(row % PREV if row < 0 else row, 1), :] + switch(g, j))
        window(g, earlier, False)

    arrived(all_squares, square_send, square_recv, no - 1).wait_recv()
    row_squares = jnp.sum(all_squares[...], axis=0)
    scale[...] = lax.rsqrt(row_squares / width + 1e-6)

    small[2].wait()
    for g in range(groups):
        rows = pl.ds(g * BLK, BLK)
        by_token = jnp.broadcast_to(scale[pl.ds(g, 1), :], (HD, BLK)).T
        for h in range(heads):
            cols = pl.ds(h * HD, HD)
            normed = lin[rows, cols] * by_token
            out[rows, cols] = (normed * gain_ref[:, cols] + local[rows, cols]).astype(jnp.bfloat16)


    @pl.when(owner)
    def _():
        arrived(total, parts_send, parts_recv.at[0], owners - 1).wait_send()

        @pl.when(first)
        def _():
            arrived(prefixes, prefix_send, prefix_recv, ni - 1).wait_send()

        @pl.when(jnp.logical_not(first))
        def _():
            arrived(prefixes, prefix_send, prefix_recv, ni - 2).wait_send()

    @pl.when(jnp.logical_not(jnp.logical_or(owner, last)))
    def _():
        arrived(total, parts_send, parts_recv.at[0], owners).wait_send()

    arrived(all_squares, square_send, square_recv, no - 1).wait_send()

    @pl.when(jnp.logical_not(last))
    def _():
        for n, (source, target, _) in enumerate(rims):
            push(n, source, target, rim_send, rim_recv, following).wait_send()

    @pl.when(relays)
    def _():
        for n, (_, target, relay) in enumerate(rims):
            push(n, relay, target, hop_send, rim_recv, head).wait_send()


def shards(ni, no, queries, keys, values, counts, window_mask, norm_gain):
    span, wide = queries.shape
    groups, heads = span // BLK, wide // HD
    owners = ni // 2
    piece = heads * HD // owners
    rim = PREV * BLK
    any_space = pl.BlockSpec(memory_space=pltpu.HBM)
    dma = pltpu.SemaphoreType.DMA
    f32, bf16 = jnp.float32, jnp.bfloat16
    return pl.pallas_call(
        functools.partial(kernel, ni, no, groups, heads),
        out_shape=jax.ShapeDtypeStruct((span, wide), bf16),
        in_specs=[any_space] * 6,
        out_specs=pl.BlockSpec(memory_space=pltpu.VMEM),
        scratch_shapes=[
            pltpu.SMEM(counts.shape, jnp.int32),
            pltpu.SMEM(window_mask.shape[::-1], jnp.int32),
            pltpu.VMEM((1, wide), f32),
            pltpu.VMEM((span, wide), bf16),
            pltpu.VMEM((rim + span, wide), bf16),
            pltpu.VMEM((rim + span, wide), bf16),
            pltpu.VMEM((groups, heads * HD, HD), bf16),
            pltpu.VMEM((owners, piece, HD), bf16),
            pltpu.VMEM((ni, piece, HD), bf16),
            pltpu.VMEM((ni, piece, HD), bf16),
            pltpu.VMEM((owners, piece, HD), bf16),
            pltpu.VMEM((groups, BLK), f32),
            pltpu.VMEM((8, BLK), f32),
            pltpu.VMEM((8, BLK), f32),
            pltpu.VMEM((span, wide), f32),
            pltpu.VMEM((span, wide), f32),
            pltpu.VMEM((groups, BLK), f32),
            pltpu.VMEM((no, groups, BLK), f32),
            pltpu.VMEM((groups, BLK), f32),
            dma((3,)),
            dma((2 * LOADS + 1,)),
            dma,
            dma((ni // max(1, ni // 8),)),
            dma,
            dma,
            dma((2 * PREV + 1,)),
            dma((2 * PREV + 1,)),
            dma,
            dma,
            pltpu.SemaphoreType.REGULAR,
            pltpu.SemaphoreType.REGULAR,
            pltpu.SemaphoreType.REGULAR,
            pltpu.VMEM((8, BLK), f32),
            pltpu.VMEM((rim, wide), bf16),
            pltpu.VMEM((rim, wide), bf16),
            dma((2 * PREV + 1,)),
            dma((2 * PREV + 1,)),
        ],
        compiler_params=pltpu.CompilerParams(
            collective_id=0, has_side_effects=True, vmem_limit_bytes=40 * 2**20
        ),
        name="layer",
    )(*(pltpu.with_memory_space_constraint(x, pltpu.HBM) for x in (counts, window_mask.T, norm_gain.reshape(1, wide), queries, keys, values)))


def solution(mesh):
    return jax.shard_map(
        functools.partial(shards, mesh.shape["inner"], mesh.shape["outer"]),
        mesh=mesh,
        in_specs=(
            P("inner", "outer"),
            P("inner", "outer"),
            P("inner", "outer"),
            P("inner"),
            P("inner", None),
            P("outer"),
        ),
        out_specs=P("inner", "outer"),
        check_vma=False,
    )
```

```python
import functools

import jax
import jax.numpy as jnp
from jax import lax
from jax.experimental import pallas as pl
from jax.experimental.pallas import tpu as pltpu
from jax.sharding import PartitionSpec as P

HD = 128
BLK = 128
PREV = 3
LOADS = 2
MESH = pl.DeviceIdType.MESH
NEG = -1e30
LOG2E = 1.4426950408889634


def far_first(size):
    return sorted(range(size), key=lambda s: min(s, size - s), reverse=True)


def dot_nt(a, b):
    return lax.dot_general(a, b, (((1,), (1,)), ((), ())), preferred_element_type=jnp.float32)


def dot_tn(a, b):
    return lax.dot_general(a, b, (((0,), (0,)), ((), ())), preferred_element_type=jnp.float32)


def dot_nn(a, b):
    return lax.dot_general(a, b, (((1,), (0,)), ((), ())), preferred_element_type=jnp.float32)


def kernel(
    ni,
    no,
    groups,
    heads,
    counts_hbm,
    mask_hbm,
    gain_hbm,
    q_hbm,
    k_hbm,
    v_hbm,
    out,
    counts_ref,
    mask_ref,
    gain_ref,
    q_all,
    k_ext,
    v_ext,
    within,
    total,
    parts,
    prefixes,
    before,
    bias,
    rim_out,
    rim_in,
    lin,
    local,
    squares,
    all_squares,
    scale,
    small_sem,
    load_sem,
    parts_send,
    parts_recv,
    prefix_send,
    prefix_recv,
    rim_send,
    rim_recv,
    square_send,
    square_recv,
    ready,
    entered,
    go,
    relay_bias,
    relay_keys,
    relay_values,
    hop_send,
    hop_recv,
):
    rim = PREV * BLK
    span = groups * BLK
    width = no * heads * HD
    here = lax.axis_index("inner")
    stripe = lax.axis_index("outer")
    following = lax.rem(here + 1, ni)

    small = [
        pltpu.make_async_copy(counts_hbm, counts_ref, small_sem.at[0]),
        pltpu.make_async_copy(mask_hbm, mask_ref, small_sem.at[1]),
        pltpu.make_async_copy(gain_hbm, gain_ref, small_sem.at[2]),
    ]
    chunk = span // LOADS
    loads = []
    for n in range(LOADS):
        rows, ext = pl.ds(n * chunk, chunk), pl.ds(rim + n * chunk, chunk)
        loads.append(pltpu.make_async_copy(k_hbm.at[rows], k_ext.at[ext], load_sem.at[2 * n]))
        loads.append(pltpu.make_async_copy(v_hbm.at[rows], v_ext.at[ext], load_sem.at[2 * n + 1]))
    load_q = pltpu.make_async_copy(q_hbm, q_all, load_sem.at[2 * LOADS])
    small[0].start()
    for load in loads:
        load.start()
    small[1].start()
    small[2].start()
    load_q.start()

    barrier = pltpu.get_barrier_semaphore()
    inner_sizes = {32: (4, 8), 8: (2, 4)}.get(ni, (1, ni))
    outer_sizes = (8, 2) if no == 16 else (no, 1)
    rows_of_chips, line = inner_sizes
    layers, cores = outer_sizes
    half = line // 2
    owners = ni // 2

    def owns(place):
        return lax.rem(place, line) < half

    def rank(place):
        return lax.div(place, line) * half + lax.rem(place, line)

    owner = owns(here)
    preceding = lax.rem(here + ni - 1, ni)
    first, last = here == 0, here == ni - 1
    tail = lax.rem(here, line) == line - 1
    straight = jnp.logical_not(tail)
    detour = jnp.logical_and(tail, jnp.logical_not(last))
    relays = jnp.logical_and(tail, here >= line)
    ahead = lax.rem(here + line, ni)
    behind = lax.rem(here + ni - line, ni)
    along, across = lax.rem(here, line), lax.div(here, line)
    head = across * line
    rows_far_first = [
        (dx, lax.rem(across + dx, rows_of_chips) * line) for dx in far_first(rows_of_chips)
    ]
    tall, deep = lax.div(stripe, cores), lax.rem(stripe, cores)

    def to_outer(act):
        for dy in far_first(layers):
            base = lax.rem(tall + dy, layers) * cores
            for dc in range(cores):
                if dy or dc:
                    act({"outer": base + lax.rem(deep + dc, cores)})

    def to_inner(act, only_owners):
        for dz in far_first(line):
            z = lax.rem(along + dz, line)

            def send(dz=dz, z=z):
                for dx, row in rows_far_first:
                    if dx or dz:
                        act(row + z, lax.div(row, 2) + z)

            if only_owners:
                pl.when(z < half)(send)
            else:
                send()

    def greet(peer):
        pl.semaphore_signal(barrier, inc=1, device_id=peer, device_id_type=MESH)

    @pl.when(owner)
    def _():
        to_inner(lambda there, _: greet({"inner": there}), False)

    @pl.when(jnp.logical_not(owner))
    def _():
        pl.semaphore_signal(barrier, inc=1, device_id={"inner": preceding}, device_id_type=MESH)

    @pl.when(relays)
    def _():
        pl.semaphore_signal(barrier, inc=1, device_id={"inner": behind}, device_id_type=MESH)

    hub = stripe == 0

    @pl.when(hub)
    def _():
        to_outer(greet)

    small[0].wait()
    lane = lax.broadcasted_iota(jnp.int32, (1, BLK), 1)
    for g in range(groups):
        bias[pl.ds(g, 1), :] = jnp.where(lane < counts_ref[g], 0.0, NEG)
    rim_out[...] = jnp.full(rim_out.shape, NEG, jnp.float32)
    for j in range(PREV):
        rim_out[pl.ds(j, 1), :] = bias[pl.ds(groups - PREV + j, 1), :]

    greeters = (
        owners
        - jnp.where(owner, 1, 0)
        + jnp.where(owns(following), 0, 1)
        + jnp.where(detour, 1, 0)
        + jnp.where(hub, 0, 1)
    )
    rims = [(rim_out, rim_in, relay_bias)]
    for n in reversed(range(PREV)):
        for ext, relay in ((k_ext, relay_keys), (v_ext, relay_values)):
            near, far = pl.ds(n * BLK, BLK), pl.ds(span + n * BLK, BLK)
            rims.append((ext.at[far], ext.at[near], relay.at[near]))

    def push(n, source, target, send, recv, there):
        return pltpu.make_async_remote_copy(
            src_ref=source,
            dst_ref=target,
            send_sem=send.at[n],
            recv_sem=recv.at[n],
            device_id={"inner": there},
            device_id_type=MESH,
        )

    token = lax.broadcasted_iota(jnp.int32, (BLK, HD), 0)
    each = owners // heads
    piece = heads * HD // owners
    running = [jnp.zeros((HD, HD), jnp.float32)] * heads
    for g in range(groups):
        if (g * BLK) % chunk == 0:
            loads[2 * (g * BLK // chunk)].wait()
            loads[2 * (g * BLK // chunk) + 1].wait()
        for h in range(heads):
            cols = pl.ds(h * HD, HD)
            rows = pl.ds(rim + g * BLK, BLK)
            masked = jnp.where(token < counts_ref[g], k_ext[rows, cols], jnp.zeros((), jnp.bfloat16))
            if g:
                within[g, cols, :] = running[h].astype(jnp.bfloat16)
            running[h] = running[h] + dot_tn(masked, v_ext[rows, cols])
    for h in range(heads):
        total[pl.ds(h * each, each)] = running[h].reshape(each, piece, HD).astype(jnp.bfloat16)
    within[0] = jnp.zeros(within.shape[1:], jnp.bfloat16)

    pl.semaphore_wait(barrier, greeters)

    stage = max(1, ni // 8)
    stages = ni // stage
    my_stage = lax.div(here, stage)

    def send_part(there, place):
        pltpu.make_async_remote_copy(
            src_ref=total.at[place],
            dst_ref=parts.at[here],
            send_sem=parts_send,
            recv_sem=parts_recv.at[my_stage],
            device_id={"inner": there},
            device_id_type=MESH,
        ).start()

    @pl.when(jnp.logical_not(last))
    def _():
        to_inner(send_part, True)

    @pl.when(detour)
    def _():
        for n, (source, _, relay) in enumerate(rims):
            push(n, source, relay, rim_send, hop_recv, ahead).start()

    @pl.when(straight)
    def _():
        for n, (source, target, _) in enumerate(rims):
            push(n, source, target, rim_send, rim_recv, following).start()

    @pl.when(first)
    def _():
        rim_in[...] = jnp.full(rim_in.shape, NEG, jnp.float32)
        before[...] = jnp.zeros(before.shape, jnp.bfloat16)
        k_ext[pl.ds(0, rim)] = jnp.zeros((rim, k_ext.shape[1]), jnp.bfloat16)
        v_ext[pl.ds(0, rim)] = jnp.zeros((rim, v_ext.shape[1]), jnp.bfloat16)

    @pl.when(jnp.logical_not(hub))
    def _():
        pl.semaphore_signal(entered, inc=1, device_id={"outer": 0}, device_id_type=MESH)

    @pl.when(jnp.logical_not(owner))
    def _():
        for n in range(owners):
            pl.semaphore_signal(
                ready,
                inc=1,
                device_id={"inner": n // half * line + n % half},
                device_id_type=MESH,
            )

    load_q.wait()
    small[1].wait()
    causal = lax.broadcasted_iota(jnp.int32, (BLK, BLK), 0) >= lax.broadcasted_iota(
        jnp.int32, (BLK, BLK), 1
    )
    factor = LOG2E / HD**0.5

    def intra(g, scores, h):
        valid = causal & (bias[pl.ds(g, 1), :] == 0.0)
        weights = jnp.where(valid, scores, 0.0).astype(jnp.bfloat16)
        rows, cols = pl.ds(g * BLK, BLK), pl.ds(h * HD, HD)
        lin[rows, cols] = dot_nn(weights, v_ext[pl.ds(rim + g * BLK, BLK), cols]) + dot_nn(
            q_all[rows, cols], within[g, cols, :]
        )

    def window(g, earlier, with_intra):
        rows = pl.ds(g * BLK, BLK)
        for h in range(heads):
            cols = pl.ds(h * HD, HD)
            keys = pl.ds(g * BLK, (PREV + 1) * BLK)
            scores = dot_nt(q_all[rows, cols], k_ext[keys, cols])
            own = scores[:, PREV * BLK :]
            if with_intra:
                intra(g, own, h)
            seen = [scores[:, j * BLK : (j + 1) * BLK] + earlier[j] for j in range(PREV)]
            seen.append(jnp.where(causal, own + bias[pl.ds(g, 1), :], NEG))
            largest = functools.reduce(jnp.maximum, seen)
            largest = jnp.max(largest, axis=-1, keepdims=True)
            expd = [jnp.exp2((s - largest) * factor) for s in seen]
            denominator = jnp.sum(functools.reduce(jnp.add, expd), axis=-1, keepdims=True)
            inverse = 1.0 / denominator
            weights = jnp.concatenate([(e * inverse).astype(jnp.bfloat16) for e in expd], axis=1)
            local[rows, cols] = dot_nn(weights, v_ext[keys, cols])

    def switch(g, j):
        return jnp.where(mask_ref[PREV - 1 - j, g] == 1, 0.0, NEG)

    def inner_window(g):
        window(g, [bias[pl.ds(g - PREV + j, 1), :] + switch(g, j) for j in range(PREV)], True)

    @pl.when(relays)
    def _():
        for n, (source, target, relay) in enumerate(rims):
            push(n, source, relay, rim_send, hop_recv, ahead).wait_recv()
            push(n, relay, target, hop_send, rim_recv, head).start()

    @pl.loop(PREV, groups)
    def _(g):
        inner_window(g)

    def arrived(buffer, send, recv, count):
        return pltpu.make_async_remote_copy(
            src_ref=buffer.at[pl.ds(0, count)],
            dst_ref=buffer.at[pl.ds(0, count)],
            send_sem=send,
            recv_sem=recv,
            device_id={"inner": following},
            device_id_type=MESH,
        )

    @pl.loop(0, PREV)
    def _(g):
        for h in range(heads):
            cols = pl.ds(h * HD, HD)
            intra(
                g,
                dot_nt(q_all[pl.ds(g * BLK, BLK), cols], k_ext[pl.ds(rim + g * BLK, BLK), cols]),
                h,
            )

    def send_prefix(n):
        @pl.when(here != n)
        def _():
            pltpu.make_async_remote_copy(
                src_ref=prefixes.at[n],
                dst_ref=before.at[rank(here)],
                send_sem=prefix_send,
                recv_sem=prefix_recv,
                device_id={"inner": n},
                device_id_type=MESH,
            ).start()

    @pl.when(owner)
    def _():
        parts[pl.ds(here, 1)] = total[pl.ds(rank(here), 1)]
        so_far = jnp.zeros(parts.shape[1:], jnp.float32)
        held = []
        for n in range(stages):
            members = stage - (n == stages - 1)
            mine = my_stage == n
            for own in range(2):
                if members > own:

                    @pl.when(mine if own else jnp.logical_not(mine))
                    def _(n=n, count=members - own):
                        arrived(parts, parts_send, parts_recv.at[n], count).wait_recv()

            following_spans = range(n * stage + 1, n * stage + members + 1)
            for m in following_spans:
                so_far = so_far + parts[m - 1].astype(jnp.float32)
                prefixes[m] = so_far.astype(jnp.bfloat16)
            for m in following_spans:
                if m % line < half:
                    send_prefix(m)
            held += [m for m in following_spans if m % line >= half]
            if n == stages - 1:
                pl.semaphore_wait(ready, ni - owners)
                for m in held:
                    send_prefix(m)

        @pl.when(jnp.logical_not(first))
        def _():
            before[pl.ds(rank(here), 1)] = prefixes[pl.ds(here, 1)]

    @pl.when(hub)
    def _():
        pl.semaphore_wait(entered, no - 1)
        to_outer(
            lambda peer: pl.semaphore_signal(go, inc=1, device_id=peer, device_id_type=MESH)
        )

    @pl.when(jnp.logical_and(owner, jnp.logical_not(first)))
    def _():
        arrived(before, prefix_send, prefix_recv, owners - 1).wait_recv()

    @pl.when(jnp.logical_not(owner))
    def _():
        arrived(before, prefix_send, prefix_recv, owners).wait_recv()


    blank = jnp.zeros((HD, HD), jnp.bfloat16)
    carried = jnp.concatenate(
        [
            jnp.concatenate(
                [
                    before[pl.ds(h * each, each)].reshape(HD, HD) if h == n else blank
                    for n in range(heads)
                ],
                axis=1,
            )
            for h in range(heads)
        ],
        axis=0,
    )
    for g in range(groups):
        rows = pl.ds(g * BLK, BLK)
        whole = lin[rows, :] + dot_nn(q_all[rows, :], carried)
        lin[rows, :] = whole
        powers = whole * whole
        powers = sum(powers[:, h * HD : (h + 1) * HD] for h in range(heads))
        squares[pl.ds(g, 1), :] = jnp.sum(powers.T, axis=0, keepdims=True)

    all_squares[pl.ds(stripe, 1)] = squares[...][None]

    @pl.when(jnp.logical_not(hub))
    def _():
        pl.semaphore_wait(go, 1)


    to_outer(
        lambda peer: pltpu.make_async_remote_copy(
            src_ref=squares,
            dst_ref=all_squares.at[stripe],
            send_sem=square_send,
            recv_sem=square_recv,
            device_id=peer,
            device_id_type=MESH,
        ).start()
    )

    def rim_here(n):
        source, target, _ = rims[n]

        @pl.when(jnp.logical_not(first))
        def _():
            push(n, source, target, rim_send, rim_recv, following).wait_recv()

    rim_here(0)
    for g in reversed(range(PREV)):
        rim_here(2 * (PREV - g) - 1)
        rim_here(2 * (PREV - g))
        earlier = []
        for j in range(PREV):
            row = g - PREV + j
            source = rim_in if row < 0 else bias
            earlier.append(source[pl.ds(row % PREV if row < 0 else row, 1), :] + switch(g, j))
        window(g, earlier, False)

    arrived(all_squares, square_send, square_recv, no - 1).wait_recv()
    row_squares = jnp.sum(all_squares[...], axis=0)
    scale[...] = lax.rsqrt(row_squares / width + 1e-6)

    small[2].wait()
    for g in range(groups):
        rows = pl.ds(g * BLK, BLK)
        by_token = jnp.broadcast_to(scale[pl.ds(g, 1), :], (HD, BLK)).T
        for h in range(heads):
            cols = pl.ds(h * HD, HD)
            normed = lin[rows, cols] * by_token
            out[rows, cols] = (normed * gain_ref[:, cols] + local[rows, cols]).astype(jnp.bfloat16)


    @pl.when(owner)
    def _():
        arrived(total, parts_send, parts_recv.at[0], owners - 1).wait_send()

        @pl.when(first)
        def _():
            arrived(prefixes, prefix_send, prefix_recv, ni - 1).wait_send()

        @pl.when(jnp.logical_not(first))
        def _():
            arrived(prefixes, prefix_send, prefix_recv, ni - 2).wait_send()

    @pl.when(jnp.logical_not(jnp.logical_or(owner, last)))
    def _():
        arrived(total, parts_send, parts_recv.at[0], owners).wait_send()

    arrived(all_squares, square_send, square_recv, no - 1).wait_send()

    @pl.when(jnp.logical_not(last))
    def _():
        for n, (source, target, _) in enumerate(rims):
            push(n, source, target, rim_send, rim_recv, following).wait_send()

    @pl.when(relays)
    def _():
        for n, (_, target, relay) in enumerate(rims):
            push(n, relay, target, hop_send, rim_recv, head).wait_send()


def shards(ni, no, queries, keys, values, counts, window_mask, norm_gain):
    span, wide = queries.shape
    groups, heads = span // BLK, wide // HD
    owners = ni // 2
    piece = heads * HD // owners
    rim = PREV * BLK
    any_space = pl.BlockSpec(memory_space=pltpu.HBM)
    dma = pltpu.SemaphoreType.DMA
    f32, bf16 = jnp.float32, jnp.bfloat16
    return pl.pallas_call(
        functools.partial(kernel, ni, no, groups, heads),
        out_shape=jax.ShapeDtypeStruct((span, wide), bf16),
        in_specs=[any_space] * 6,
        out_specs=pl.BlockSpec(memory_space=pltpu.VMEM),
        scratch_shapes=[
            pltpu.SMEM(counts.shape, jnp.int32),
            pltpu.SMEM(window_mask.shape[::-1], jnp.int32),
            pltpu.VMEM((1, wide), f32),
            pltpu.VMEM((span, wide), bf16),
            pltpu.VMEM((rim + span, wide), bf16),
            pltpu.VMEM((rim + span, wide), bf16),
            pltpu.VMEM((groups, heads * HD, HD), bf16),
            pltpu.VMEM((owners, piece, HD), bf16),
            pltpu.VMEM((ni, piece, HD), bf16),
            pltpu.VMEM((ni, piece, HD), bf16),
            pltpu.VMEM((owners, piece, HD), bf16),
            pltpu.VMEM((groups, BLK), f32),
            pltpu.VMEM((8, BLK), f32),
            pltpu.VMEM((8, BLK), f32),
            pltpu.VMEM((span, wide), f32),
            pltpu.VMEM((span, wide), f32),
            pltpu.VMEM((groups, BLK), f32),
            pltpu.VMEM((no, groups, BLK), f32),
            pltpu.VMEM((groups, BLK), f32),
            dma((3,)),
            dma((2 * LOADS + 1,)),
            dma,
            dma((ni // max(1, ni // 8),)),
            dma,
            dma,
            dma((2 * PREV + 1,)),
            dma((2 * PREV + 1,)),
            dma,
            dma,
            pltpu.SemaphoreType.REGULAR,
            pltpu.SemaphoreType.REGULAR,
            pltpu.SemaphoreType.REGULAR,
            pltpu.VMEM((8, BLK), f32),
            pltpu.VMEM((rim, wide), bf16),
            pltpu.VMEM((rim, wide), bf16),
            dma((2 * PREV + 1,)),
            dma((2 * PREV + 1,)),
        ],
        compiler_params=pltpu.CompilerParams(
            collective_id=0, has_side_effects=True, vmem_limit_bytes=40 * 2**20
        ),
        name="layer",
    )(*(pltpu.with_memory_space_constraint(x, pltpu.HBM) for x in (counts, window_mask.T, norm_gain.reshape(1, wide), queries, keys, values)))


def solution(mesh):
    return jax.shard_map(
        functools.partial(shards, mesh.shape["inner"], mesh.shape["outer"]),
        mesh=mesh,
        in_specs=(
            P("inner", "outer"),
            P("inner", "outer"),
            P("inner", "outer"),
            P("inner"),
            P("inner", None),
            P("outer"),
        ),
        out_specs=P("inner", "outer"),
        check_vma=False,
    )
```
